256 devices in a mesh: visit: 32 (over z_lo, y, core), tile: 8 (over z_hi, x).
Axes of the slice: x: 4, y: 4, z: 8 (z_hi: 2, z_lo: 4; z = z_hi * 4 + z_lo), core: 2. Of those that a mesh axis runs over, the one named last changes fastest.
Arguments:
- exposures: float32 [32, 2048, 256], P('visit', 'tile'), may hold values from 0.3 to 3
- sky_model: float32 [2048, 256], P(('tile', 'visit')), may hold values from 0.5 to 2
- blur_kernels: float32 [32, 31, 31], P('visit'), may hold values from 0.05 to 1
- coverage: int32 [32, 8], P('visit'), may hold values from 0 to 1, as said below
Outputs:
- deconvolved: float32 [2048, 256], P(('tile', 'visit'))
The draws below stay inside these ranges and needn't reach their ends.
Inputs may be any that keep to these rules, and one draw needn't show every extreme that they name: `coverage`: every tile is covered by at least one exposure.
All inputs are finite; a program needn't handle non-finite values.
Results may differ from the reference program's by a relative error of at most 0.0001.
Values sent between devices are 32-bit elements; how exact they have to be, the bound alone decides.
A program may use at most 128 MiB of HBM per device.

```python
import math
import jax
import jax.numpy as jnp
from jax import lax

TILE_R = 256
TILE_C = 256
PSF = 31
ITERS = 2
EXPOSURES = 32
NTILES = 8
NROWS = 2048


def draw_coverage(key, part):
    first_key = jax.random.fold_in(key, 11)
    second_key = jax.random.fold_in(key, 23)
    levels = jax.random.randint(first_key, (EXPOSURES, NTILES), 0, 1000)
    limits = 250 + 600 * jnp.arange(EXPOSURES) // EXPOSURES
    covered = levels < limits[:, None]
    forced = jax.random.randint(second_key, (NTILES,), 0, EXPOSURES)
    covered = covered | (jnp.arange(EXPOSURES)[:, None] == forced[None, :])
    return covered.astype(jnp.int32)


def level_of(key, dims, split, smallest, largest):
    factor_of = 1.0
    for dim, shards_of in split:
        steps = jax.random.uniform(jax.random.fold_in(jax.random.fold_in(key, 6), dim), (shards_of,), jnp.float32, smallest / len(split), largest / len(split))
        factor_of = factor_of * jnp.repeat(jnp.exp(steps), dims[dim] // shards_of).reshape((-1,) + (1,) * (len(dims) - 1 - dim))
    return factor_of


def setup_inputs(seed: int = 0) -> dict:
    arg_keys = jax.random.split(jax.random.key(seed), 5)
    exposures = jnp.clip(jnp.exp(math.log(3.0) - 2.3025851 * jax.random.uniform(arg_keys[0], (EXPOSURES, NROWS, TILE_C), jnp.float32) ** level_of(arg_keys[0], (EXPOSURES, NROWS, TILE_C), ((0, 32), (1, 8)), -0.2, 0.2)), 0.3, 3.0)
    sky_model = jnp.clip(jnp.exp(math.log(2.0) - 1.3862944 * jax.random.uniform(arg_keys[1], (NROWS, TILE_C), jnp.float32) ** level_of(arg_keys[1], (NROWS, TILE_C), ((0, 256),), -0.2, 0.2)), 0.5, 2.0)
    blur_kernels = jnp.clip(jnp.exp(math.log(1.0) - 2.9957323 * jax.random.uniform(arg_keys[2], (EXPOSURES, PSF, PSF), jnp.float32) ** level_of(arg_keys[2], (EXPOSURES, PSF, PSF), ((0, 32),), -0.2, 0.2)), 0.05, 1.0)
    coverage = draw_coverage(jax.random.fold_in(arg_keys[4], 71), 0)
    return dict(exposures=exposures, sky_model=sky_model, blur_kernels=blur_kernels, coverage=coverage)


def correlate(field, kernel):
    half = kernel.shape[0] // 2
    result = lax.conv_general_dilated(field[None, None], kernel[None, None], (1, 1), [(half, half), (half, half)], precision=lax.Precision.HIGHEST)
    return result[0, 0]


def reference(exposures, sky_model, blur_kernels, coverage):
    kernels = blur_kernels / jnp.sum(blur_kernels, axis=(1, 2), keepdims=True)
    row_tile = jnp.arange(NROWS) // TILE_R
    weights = coverage.astype(jnp.float32)[:, row_tile]

    def norm_step(total, member):
        weight_row, kernel = member
        field = jnp.broadcast_to(weight_row[:, None], (NROWS, TILE_C))
        return total + correlate(field, kernel), None

    zeros_field = jnp.zeros((NROWS, TILE_C), jnp.float32)
    norm_field, _ = lax.scan(norm_step, zeros_field, (weights, kernels))
    model = sky_model
    for step in range(ITERS):
        def update_step(total, member):
            counts, weight_row, kernel = member
            blurred = correlate(model, kernel[::-1, ::-1])
            ratio = weight_row[:, None] * counts / blurred
            return total + correlate(ratio, kernel), None

        numerator, _ = lax.scan(update_step, zeros_field, (exposures, weights, kernels))
        model = model * numerator / norm_field
    return model
```

```python
import jax
import jax.numpy as jnp
from jax import lax
from jax.experimental import pallas as pl
from jax.experimental.pallas import tpu as pltpu
from jax.sharding import PartitionSpec as P

F32 = jnp.float32
BF = jnp.bfloat16
HI = lax.Precision.HIGHEST
MESH = pl.DeviceIdType.MESH
ITERS = 2


def iota(shape, dim):
    return lax.broadcasted_iota(jnp.int32, shape, dim)


def block_swap(x):
    s = iota((8, 256), 0)
    b = iota((8, 256), 1) // 32
    out = x
    for d in range(1, 8):
        moved = pltpu.roll(pltpu.roll(x, d, 0), 256 - 32 * d, 1)
        out = jnp.where((s - b) % 8 == d, moved, out)
    return out


def build_rows(k, rows):
    rows[...] = jnp.zeros_like(rows)
    m = iota((128, 128), 1)
    b = iota((128, 128), 0)
    for r in range(4):
        pick = ((m == (32 * r - 1 - b + 256) % 128) & (b < 31)).astype(F32)
        moved = jnp.dot(k, pick, precision=HI, preferred_element_type=F32)
        rows[5 + r : 37 + r, :] = rows[5 + r : 37 + r, :] + moved


def build_operator(rows, op_hi, op_lo, start, stop):
    c2 = iota((64, 128), 0)
    b = c2 - 1 - iota((64, 128), 1) % 32
    inside = (b >= 0) & (b <= 30)

    def step(j, carry):
        wide = jnp.broadcast_to(rows[pl.ds(j, 1), :], (64, 128))
        value = jnp.where(inside, pltpu.roll(wide, 0, 1, stride=1, stride_axis=0), 0.0)
        hi = value.astype(BF)
        lo = (value - hi.astype(F32)).astype(BF)
        first = pl.multiple_of(j * 64, 64)
        second = pl.multiple_of(j * 64 + 256, 64)
        op_hi[pl.ds(first, 64), 0:128] = hi
        op_lo[pl.ds(first, 64), 0:128] = lo
        op_hi[pl.ds(second, 64), 128:256] = hi
        op_lo[pl.ds(second, 64), 128:256] = lo
        return carry

    lax.fori_loop(start, stop, step, 0)


def windows(v):
    n = v.shape[0]
    group = iota(v.shape, 0) % 8
    lane = iota(v.shape, 1)
    before = jnp.where(group > 0, pltpu.roll(v, 1, 0), 0.0)
    after = jnp.where(group < 7, pltpu.roll(v, n - 1, 0), 0.0)

    def pair(mid0, left0, right0, mid1, left1, right1):
        out = jnp.where(lane < 16, pltpu.roll(before, left0, 1), pltpu.roll(v, mid0, 1))
        out = jnp.where(lane >= 48, pltpu.roll(after, right0, 1), out)
        out = jnp.where(lane >= 64, pltpu.roll(before, left1, 1), out)
        out = jnp.where(lane >= 80, pltpu.roll(v, mid1, 1), out)
        return jnp.where(lane >= 112, pltpu.roll(after, right1, 1), out)

    return pair(16, 112, 48, 48, 16, 80), pair(80, 48, 112, 112, 80, 16)


def put_windows(value, first_block, wide):
    rows = value.shape[0]
    at = pl.multiple_of(first_block * 8, 8)
    for q in range(2):
        one, two = windows(value[:, 128 * q : 128 * q + 128])
        wide[q, pl.ds(at, rows), 0:128] = one
        wide[q, pl.ds(at, rows), 128:256] = two


def product(wide, m, x_hi, x_lo, op_hi, op_lo):
    for part in range(10):
        value = wide[part % 2, (part // 2) * 8 : (part // 2) * 8 + m, :]
        hi = value.astype(BF)
        x_hi[0:m, 256 * part : 256 * part + 256] = hi
        x_lo[0:m, 256 * part : 256 * part + 256] = (value - hi.astype(F32)).astype(BF)

    def dot(x, op):
        return jnp.dot(x[0:m, :], op[256 : 256 + 2560, :], preferred_element_type=F32)

    return dot(x_hi, op_hi) + (dot(x_hi, op_lo) + dot(x_lo, op_hi))


def kernel(
    exp_ref, sky_ref, ker_ref, cov_ref, out_ref,
    kpad, rows, fwd_hi, fwd_lo, flip_hi, flip_lo, wide, x_hi, x_lo,
    own, prev, follow, exp_prev, exp_follow, expo, ratio, norm,
    q_sum, q_in, nums, r_core, a_sum, r_y, b_sum, r_z,
    ag_send, ag_recv, rs_send, rs_recv, q_send, q_recv, e_send, e_recv,
):
    t = lax.axis_index("tile")
    v = lax.axis_index("visit")
    tiles = lax.axis_size("tile")
    z, y, c = v // 8, (v // 2) % 4, v % 2

    def at_z(z2):
        return {"visit": z2 * 8 + y * 2 + c, "tile": t}

    def at_y(y2):
        return {"visit": z * 8 + y2 * 2 + c, "tile": t}

    partner = {"visit": z * 8 + y * 2 + (1 - c), "tile": t}
    up = {"visit": v, "tile": t + 1}
    down = {"visit": v, "tile": t - 1}
    has_up = t < tiles - 1
    has_down = t > 0

    barrier = pltpu.get_barrier_semaphore()
    peers = [at_z((z + d) % 4) for d in (1, 2, 3)] + [at_y((y + d) % 4) for d in (1, 2, 3)] + [partner]
    for peer in peers:
        pl.semaphore_signal(barrier, inc=1, device_id=peer, device_id_type=MESH)

    @pl.when(has_up)
    def _():
        pl.semaphore_signal(barrier, inc=1, device_id=up, device_id_type=MESH)

    @pl.when(has_down)
    def _():
        pl.semaphore_signal(barrier, inc=1, device_id=down, device_id_type=MESH)

    def remote(src, dst, send, recv, device):
        return pltpu.make_async_remote_copy(
            src_ref=src, dst_ref=dst, send_sem=send, recv_sem=recv, device_id=device, device_id_type=MESH
        )

    prev[...] = jnp.zeros_like(prev)
    follow[...] = jnp.zeros_like(follow)
    kpad[...] = jnp.zeros_like(kpad)
    raw = ker_ref[0]
    kpad[0:31, 0:31] = raw / jnp.sum(raw)
    own[0, z, y, c] = block_swap(sky_ref[...])
    w_here = cov_ref[0, t].astype(F32)
    w_down = jnp.where(has_down, cov_ref[0, jnp.maximum(t - 1, 0)], 0).astype(F32)
    w_up = jnp.where(has_up, cov_ref[0, jnp.minimum(t + 1, tiles - 1)], 0).astype(F32)
    edge = iota((32, 32), 0) + iota((32, 32), 1)
    weights = jnp.where(edge < 15, w_down, jnp.where(edge >= 46, w_up, w_here))
    q_sum[0] = jnp.dot(weights, kpad[...], precision=HI, preferred_element_type=F32)

    turn_rows = (iota((32, 32), 0) + iota((32, 32), 1) == 30).astype(F32)
    turn_cols = (iota((128, 128), 0) + iota((128, 128), 1) == 30).astype(F32)
    turned = jnp.dot(turn_rows, kpad[...], precision=HI, preferred_element_type=F32)
    turned = jnp.dot(turned, turn_cols, precision=HI, preferred_element_type=F32)
    build_rows(turned, rows)
    build_operator(rows, flip_hi, flip_lo, 0, 44)

    count = 7 + has_up.astype(jnp.int32) + has_down.astype(jnp.int32)
    pl.semaphore_wait(barrier, count)

    def send_exposures(act):
        @pl.when(has_up)
        def _():
            act(remote(exp_ref.at[0, 240:256, :], exp_prev, e_send.at[0], e_recv.at[0], up))

        @pl.when(has_down)
        def _():
            act(remote(exp_ref.at[0, 0:16, :], exp_follow, e_send.at[1], e_recv.at[1], down))

    def recv_exposures():
        @pl.when(has_down)
        def _():
            remote(exp_ref.at[0, 240:256, :], exp_prev, e_send.at[0], e_recv.at[0], down).wait_recv()

        @pl.when(has_up)
        def _():
            remote(exp_ref.at[0, 0:16, :], exp_follow, e_send.at[1], e_recv.at[1], up).wait_recv()

    def halo_up(it, device):
        return remote(own.at[it, 3, 2:4], prev.at[it], ag_send.at[it, 7], ag_recv.at[it, 7], device)

    def halo_down(it, device):
        return remote(own.at[it, 0, 0:2], follow.at[it], ag_send.at[it, 8], ag_recv.at[it, 8], device)

    def send_halo(it, act):
        @pl.when(has_up)
        def _():
            act(halo_up(it, up))

        @pl.when(has_down)
        def _():
            act(halo_down(it, down))

    def recv_halo(it):
        @pl.when(has_down)
        def _():
            halo_up(it, down).wait_recv()

        @pl.when(has_up)
        def _():
            halo_down(it, up).wait_recv()

    pending = []

    def start(copies):
        for copy in copies:
            copy.start()
        pending.extend(copies)
        return copies

    def gather_z(it):
        part = own.at[it, z, y, c]
        return [remote(part, part, ag_send.at[it, d - 1], ag_recv.at[it, d - 1], at_z((z + d) % 4)) for d in (1, 2, 3)]

    def gather_y(it):
        part = own.at[it, :, y, c]
        return [remote(part, part, ag_send.at[it, d + 2], ag_recv.at[it, d + 2], at_y((y + d) % 4)) for d in (1, 2, 3)]

    def gather_core(it):
        part = own.at[it, :, :, c]
        return [remote(part, part, ag_send.at[it, 6], ag_recv.at[it, 6], partner)]

    def q_copies(stage, devices, base):
        return [
            remote(q_sum.at[stage], q_in.at[base + i], q_send.at[base + i], q_recv.at[base + i], device)
            for i, device in enumerate(devices)
        ]

    def arrive(copies):
        for copy in copies:
            copy.wait_recv()

    stage = start(gather_z(0) + q_copies(0, [at_z((z + d) % 4) for d in (1, 2, 3)], 0))
    send_exposures(lambda copy: copy.start())
    build_rows(kpad[...], rows)
    build_operator(rows, fwd_hi, fwd_lo, 0, 30)
    arrive(stage)
    q_sum[1] = q_sum[0] + q_in[0] + q_in[1] + q_in[2]
    stage = start(gather_y(0) + q_copies(1, [at_y((y + d) % 4) for d in (1, 2, 3)], 3))
    build_operator(rows, fwd_hi, fwd_lo, 30, 44)

    def swap_exposure(i, carry):
        for j in range(4):
            first = pl.multiple_of(32 * i + 8 * j, 8)
            expo[4 * i + j + 2] = block_swap(exp_ref[0, pl.ds(first, 8), :])
        return carry

    lax.fori_loop(0, 8, swap_exposure, 0)
    arrive(stage)
    q_sum[2] = q_sum[1] + q_in[3] + q_in[4] + q_in[5]
    stage = start(gather_core(0) + q_copies(2, [partner], 6))
    recv_exposures()
    for i in range(2):
        expo[i] = block_swap(exp_prev[8 * i : 8 * i + 8, :])
        expo[34 + i] = block_swap(exp_follow[8 * i : 8 * i + 8, :])
    arrive(stage)

    for it in range(ITERS):
        if it > 0:
            stage = start(gather_z(it))
            arrive(stage)
            stage = start(gather_y(it))
            arrive(stage)
            stage = start(gather_core(it))
            arrive(stage)
        send_halo(it, lambda copy: copy.start())
        if it == 0:
            q_sum[3] = q_sum[2] + q_in[6]
            lines = []
            for s in range(8):
                r = 8 * v + s
                line = jnp.where(r < 15, r, jnp.where(r > 240, r - 225, 15))
                lines.append(q_sum[3, pl.ds(line, 1), :])
            cover = iota((128, 256), 1) + iota((128, 256), 0) - 15
            valid = ((cover >= 0) & (cover < 256) & (iota((128, 256), 0) < 31)).astype(F32)
            field = jnp.dot(jnp.concatenate(lines, axis=0), valid, precision=HI, preferred_element_type=F32)
            norm[...] = block_swap(field)

        def own_windows(i, carry, it=it):
            zz, yy = i // 2, (i % 2) * 2
            put_windows(own[it, zz, pl.ds(yy, 2)].reshape(32, 256), 4 + 4 * i, wide)
            return carry

        lax.fori_loop(0, 8, own_windows, 0)
        recv_halo(it)
        put_windows(prev[it].reshape(32, 256), 0, wide)
        put_windows(follow[it].reshape(32, 256), 36, wide)
        blurred = product(wide, 288, x_hi, x_lo, flip_hi, flip_lo)

        for i, (low, high, weight, there) in enumerate(
            ((0, 2, w_down, has_down), (2, 34, w_here, None), (34, 36, w_up, has_up))
        ):
            part = weight * expo[low:high].reshape((high - low) * 8, 256) / blurred[low * 8 : high * 8]
            if there is not None:
                part = jnp.where(there, part, 0.0)
            ratio[low:high] = part.reshape(high - low, 8, 256)

        def ratio_windows(i, carry):
            put_windows(ratio[pl.ds(4 * i, 4)].reshape(32, 256), 4 * i, wide)
            return carry

        lax.fori_loop(0, 9, ratio_windows, 0)
        nums[it] = product(wide, 256, x_hi, x_lo, fwd_hi, fwd_lo).reshape(4, 4, 2, 8, 256)

        stage = start([remote(nums.at[it, :, :, 1 - c], r_core.at[it], rs_send.at[it, 0], rs_recv.at[it, 0], partner)])
        arrive(stage)
        a_sum[it] = nums[it, :, :, c] + r_core[it]
        stage = start(
            [
                remote(
                    a_sum.at[it, :, (y + d) % 4], r_y.at[it, d - 1],
                    rs_send.at[it, d], rs_recv.at[it, d], at_y((y + d) % 4),
                )
                for d in (1, 2, 3)
            ]
        )
        arrive(stage)
        b_sum[it] = a_sum[it, :, y] + r_y[it, 0] + r_y[it, 1] + r_y[it, 2]
        stage = start(
            [
                remote(
                    b_sum.at[it, (z + d) % 4], r_z.at[it, d - 1],
                    rs_send.at[it, d + 3], rs_recv.at[it, d + 3], at_z((z + d) % 4),
                )
                for d in (1, 2, 3)
            ]
        )
        arrive(stage)
        total = b_sum[it, z] + r_z[it, 0] + r_z[it, 1] + r_z[it, 2]
        model = own[it, z, y, c] * total / norm[...]
        if it < ITERS - 1:
            own[it + 1, z, y, c] = model
        else:
            out_ref[...] = block_swap(model)

    for copy in pending:
        copy.wait_send()
    send_exposures(lambda copy: copy.wait_send())
    for it in range(ITERS):
        send_halo(it, lambda copy: copy.wait_send())


def body(exposures, sky_model, blur_kernels, coverage):
    vmem = pl.BlockSpec(memory_space=pltpu.VMEM)
    V = pltpu.VMEM
    D = pltpu.SemaphoreType.DMA
    return pl.pallas_call(
        kernel,
        out_shape=jax.ShapeDtypeStruct((8, 256), F32),
        in_specs=[vmem, vmem, vmem, pl.BlockSpec(memory_space=pltpu.SMEM)],
        out_specs=vmem,
        scratch_shapes=[
            V((32, 128), F32), V((48, 128), F32),
            V((3072, 256), BF), V((3072, 256), BF), V((3072, 256), BF), V((3072, 256), BF),
            V((2, 320, 256), F32), V((288, 2560), BF), V((288, 2560), BF),
            V((2, 4, 4, 2, 8, 256), F32), V((2, 2, 2, 8, 256), F32), V((2, 2, 2, 8, 256), F32),
            V((16, 256), F32), V((16, 256), F32), V((36, 8, 256), F32), V((36, 8, 256), F32), V((8, 256), F32),
            V((4, 32, 128), F32), V((7, 32, 128), F32),
            V((2, 4, 4, 2, 8, 256), F32), V((2, 4, 4, 8, 256), F32), V((2, 4, 4, 8, 256), F32),
            V((2, 3, 4, 8, 256), F32), V((2, 4, 8, 256), F32), V((2, 3, 8, 256), F32),
            D((2, 9)), D((2, 9)), D((2, 7)), D((2, 7)), D((7,)), D((7,)), D((2,)), D((2,)),
        ],
        compiler_params=pltpu.CompilerParams(collective_id=0, has_side_effects=True),
    )(exposures, sky_model, blur_kernels, coverage)


def solution(mesh):
    return jax.shard_map(
        body,
        mesh=mesh,
        in_specs=(
            P("visit", "tile", None),
            P(("tile", "visit"), None),
            P("visit", None, None),
            P("visit", None),
        ),
        out_specs=P(("tile", "visit"), None),
        check_vma=False,
    )
```

```python
import jax
import jax.numpy as jnp
from jax import lax
from jax.experimental import pallas as pl
from jax.experimental.pallas import tpu as pltpu
from jax.sharding import PartitionSpec as P

F32 = jnp.float32
BF = jnp.bfloat16
HI = lax.Precision.HIGHEST
MESH = pl.DeviceIdType.MESH
ITERS = 2


def iota(shape, dim):
    return lax.broadcasted_iota(jnp.int32, shape, dim)


def block_swap(x):
    s = iota((8, 256), 0)
    b = iota((8, 256), 1) // 32
    out = x
    for d in range(1, 8):
        moved = pltpu.roll(pltpu.roll(x, d, 0), 256 - 32 * d, 1)
        out = jnp.where((s - b) % 8 == d, moved, out)
    return out


def build_rows(k, rows):
    rows[...] = jnp.zeros_like(rows)
    m = iota((128, 128), 1)
    b = iota((128, 128), 0)
    for r in range(4):
        pick = ((m == (32 * r - 1 - b + 256) % 128) & (b < 31)).astype(F32)
        moved = jnp.dot(k, pick, precision=HI, preferred_element_type=F32)
        rows[5 + r : 37 + r, :] = rows[5 + r : 37 + r, :] + moved


def build_operator(rows, op_hi, op_lo):
    c2 = iota((64, 128), 0)
    b = c2 - 1 - iota((64, 128), 1) % 32
    inside = (b >= 0) & (b <= 30)

    def step(j, carry):
        wide = jnp.broadcast_to(rows[pl.ds(j, 1), :], (8, 128))
        base = pltpu.roll(wide, 0, 1, stride=1, stride_axis=0)
        value = jnp.concatenate([base] + [pltpu.roll(base, 8 * i, 1) for i in range(1, 8)], axis=0)
        value = jnp.where(inside, value, 0.0)
        hi = value.astype(BF)
        lo = (value - hi.astype(F32)).astype(BF)
        for shift, lanes in ((4, slice(0, 128)), (8, slice(128, 256))):
            o, r = (j + shift) // 8, (j + shift) % 8
            for op, x in ((op_hi, hi), (op_lo, lo)):
                op[o, 0, r, :, lanes] = x[16:48]
                op[o, 1, r, 0:16, lanes] = x[48:64]
                op[o, 1, r, 16:32, lanes] = x[0:16]
        return carry

    lax.fori_loop(0, 44, step, 0, unroll=11)


def put_near(value, first, near):
    n = value.shape[0]
    group = iota(value.shape, 0) % 8
    before = jnp.where(group > 0, pltpu.roll(value, 1, 0), 0.0)
    after = jnp.where(group < 7, pltpu.roll(value, n - 1, 0), 0.0)
    near[first : first + n, :] = jnp.where(iota(value.shape, 1) % 32 < 16, after, before)


def product(mid, near, ranges, x_hi, x_lo, op_hi, op_lo):
    row = 0
    for first, count in ranges:
        m = 8 * count
        for o in range(5):
            for k, src in ((0, mid), (1, near)):
                value = src[(first + o) * 8 : (first + o) * 8 + m, :]
                hi = value.astype(BF)
                at = 512 * o + 256 * k
                x_hi[row : row + m, at : at + 256] = hi
                x_lo[row : row + m, at : at + 256] = (value - hi.astype(F32)).astype(BF)
        row += m

    def dot(x, op):
        return jnp.dot(x[0:row, :], op[1:6].reshape(2560, 256), preferred_element_type=F32)

    return dot(x_hi, op_hi) + (dot(x_hi, op_lo) + dot(x_lo, op_hi))


def far(d):
    return -(d[0] + (2 if d[1] == 2 else 1 if d[1] else 0))


AWAY = sorted([(dz, dy) for dz in range(4) for dy in range(4) if (dz, dy) != (0, 0)], key=far)


def kernel(
    exp_hbm, sky_ref, ker_ref, cov_ref, out_ref,
    exp_ref, kpad, rows, fwd_hi, fwd_lo, flip_hi, flip_lo, mid, near, rmid, rnear, x_hi, x_lo,
    own, prev, follow, exp_prev, exp_follow, expo,
    q_all, q_core, q_sum, q_in, nums, r_core, a_sum, r_in,
    exp_sem, ag_send, ag_recv, cf_send, cf_recv, hx_send, hx_recv, hr_send, hr_recv, hc_send, hc_recv,
    rc_send, rc_recv, rs_send, rs_recv, q_send, q_recv, e_send, e_recv,
):
    t = lax.axis_index("tile")
    v = lax.axis_index("visit")
    tiles = lax.axis_size("tile")
    z, y, c = v // 8, (v // 2) % 4, v % 2
    u = v // 2

    def there(d):
        return {"visit": ((z + d[0]) % 4) * 8 + ((y + d[1]) % 4) * 2 + c, "tile": t}

    partner = {"visit": 2 * u + (1 - c), "tile": t}
    up = {"visit": v, "tile": t + 1}
    down = {"visit": v, "tile": t - 1}
    has_up = t < tiles - 1
    has_down = t > 0

    prev[...] = jnp.zeros_like(prev)
    follow[...] = jnp.zeros_like(follow)
    barrier = pltpu.get_barrier_semaphore()
    for peer in [there(d) for d in AWAY] + [partner]:
        pl.semaphore_signal(barrier, inc=1, device_id=peer, device_id_type=MESH)

    @pl.when(has_up)
    def _():
        pl.semaphore_signal(barrier, inc=1, device_id=up, device_id_type=MESH)

    @pl.when(has_down)
    def _():
        pl.semaphore_signal(barrier, inc=1, device_id=down, device_id_type=MESH)

    load = pltpu.make_async_copy(exp_hbm.at[0], exp_ref, exp_sem)
    load.start()

    def remote(src, dst, send, recv, device):
        return pltpu.make_async_remote_copy(
            src_ref=src, dst_ref=dst, send_sem=send, recv_sem=recv, device_id=device, device_id_type=MESH
        )

    sent = []

    def start(copies):
        for copy in copies:
            copy.start()
        sent.extend(copies)
        return copies

    def arrive(copies):
        for copy in copies:
            copy.wait_recv()

    def when(cond, act):
        pl.when(cond)(act)

    own[0, u, c] = block_swap(sky_ref[...])
    kpad[...] = jnp.zeros_like(kpad)
    raw = ker_ref[:, 0, :]
    kpad[0:31, 0:31] = raw / jnp.sum(raw)
    w_here = cov_ref[0, t].astype(F32)
    w_down = jnp.where(has_down, cov_ref[0, jnp.maximum(t - 1, 0)], 0).astype(F32)
    w_up = jnp.where(has_up, cov_ref[0, jnp.minimum(t + 1, tiles - 1)], 0).astype(F32)
    edge = iota((32, 32), 0) + iota((32, 32), 1)
    weights = jnp.where(edge < 15, w_down, jnp.where(edge >= 46, w_up, w_here))
    lines = jnp.dot(weights, kpad[...], precision=HI, preferred_element_type=F32)
    for owner in range(32):
        if owner < 2:
            piece = lines[8 * owner : 8 * owner + 8]
        elif owner >= 30:
            piece = lines[8 * owner - 225 : 8 * owner - 217]
        else:
            piece = jnp.broadcast_to(lines[15:16], (8, 128))
        q_all[owner // 2, owner % 2] = piece

    pl.semaphore_wait(barrier, 16 + has_up.astype(jnp.int32) + has_down.astype(jnp.int32))

    def edge_up(device):
        return remote(exp_ref.at[240:256, :], exp_prev, e_send.at[0], e_recv.at[0], device)

    def edge_down(device):
        return remote(exp_ref.at[0:16, :], exp_follow, e_send.at[1], e_recv.at[1], device)

    def hop_up(it, device):
        return remote(own.at[it, u, c], prev.at[it, u % 2, c], hx_send.at[it, 0], hx_recv.at[it, 0], device)

    def hop_down(it, device):
        return remote(own.at[it, u, c], follow.at[it, u % 2, c], hx_send.at[it, 1], hx_recv.at[it, 1], device)

    last = u >= 14
    first = u < 2

    def relay(it, which):
        buf = (prev, follow)[which].at[it, u % 2, c]
        recv = hr_recv.at[it, which, u % 2]
        return [remote(buf, buf, hr_send.at[it, which, i], recv, there(d)) for i, d in enumerate(AWAY)]

    def relayed(it, which, j):
        buf = (prev, follow)[which].at[it, j, c]
        return remote(buf, buf, hr_send.at[it, which, 0], hr_recv.at[it, which, j], partner)

    def pass_halo(it, which):
        buf = (prev, follow)[which].at[it, :, c]
        return remote(buf, buf, hc_send.at[it, which], hc_recv.at[it, which], partner)

    for it in range(ITERS):
        mine = own.at[it, u, c]
        when(last & has_up, lambda: hop_up(it, up).start())
        when(first & has_down, lambda: hop_down(it, down).start())
        gather = start(
            [remote(mine, mine, ag_send.at[it, i], ag_recv.at[it, i], there(d)) for i, d in enumerate(AWAY)]
        )
        if it == 0:
            q_swap = start([remote(q_all.at[:, 1 - c], q_core, q_send.at[15], q_recv.at[15], partner)])
            load.wait()
            when(has_up, lambda: edge_up(up).start())
            when(has_down, lambda: edge_down(down).start())
            turn_rows = (iota((32, 32), 0) + iota((32, 32), 1) == 30).astype(F32)
            turn_cols = (iota((128, 128), 0) + iota((128, 128), 1) == 30).astype(F32)
            turned = jnp.dot(turn_rows, kpad[...], precision=HI, preferred_element_type=F32)
            turned = jnp.dot(turned, turn_cols, precision=HI, preferred_element_type=F32)
            build_rows(turned, rows)
            build_operator(rows, flip_hi, flip_lo)

        def relay_up():
            hop_up(it, down).wait_recv()
            for copy in relay(it, 0):
                copy.start()

        def relay_down():
            hop_down(it, up).wait_recv()
            for copy in relay(it, 1):
                copy.start()

        when(last & has_down, relay_up)
        when(first & has_up, relay_down)
        if it == 0:
            build_rows(kpad[...], rows)
            build_operator(rows, fwd_hi, fwd_lo)

            def swap_exposure(i, carry):
                for j in range(4):
                    at = pl.multiple_of(32 * i + 8 * j, 8)
                    expo[4 * i + j + 2] = block_swap(exp_ref[pl.ds(at, 8), :])
                return carry

            lax.fori_loop(0, 8, swap_exposure, 0)

        handed = []
        for dz in range(4):
            for i, d in enumerate(AWAY):
                if d[0] == dz:
                    gather[i].wait_recv()
            part = own.at[it, pl.ds(((z - dz) % 4) * 4, 4), c]
            handed += start([remote(part, part, cf_send.at[it, dz], cf_recv.at[it, dz], partner)])
        if it == 0:
            arrive(q_swap)
            q_sum[...] = q_all[:, c] + q_core[...]
            q_spread = start(
                [
                    remote(
                        q_sum.at[((z + d[0]) % 4) * 4 + (y + d[1]) % 4], q_in.at[i], q_send.at[i], q_recv.at[i], there(d)
                    )
                    for i, d in enumerate(AWAY)
                ]
            )
        arrive(handed)

        for g in range(4):
            value = own[it, 4 * g : 4 * g + 4].reshape(64, 256)
            mid[32 + 64 * g : 96 + 64 * g, :] = value
            put_near(value, 32 + 64 * g, near)
        blurred = product(mid, near, ((4, 28),), x_hi, x_lo, flip_hi, flip_lo)
        value = w_here * expo[4:32].reshape(224, 256) / blurred
        rmid[32:256, :] = value
        for g in range(7):
            put_near(value[32 * g : 32 * g + 32], 32 + 32 * g, rnear)

        for which, comes, relayer in ((0, has_down, last), (1, has_up, first)):
            for j in range(2):
                when(
                    comes & jnp.logical_not(relayer & (u % 2 == j)),
                    lambda which=which, j=j: relayed(it, which, j).wait_recv(),
                )
            when(comes, lambda which=which: pass_halo(it, which).start())

        found = product(rmid, rnear, ((4, 24),), x_hi, x_lo, fwd_hi, fwd_lo)
        nums[it, 2:14] = found.reshape(12, 2, 8, 256)
        swap = start([remote(nums.at[it, 2:14, 1 - c], r_core.at[it, 2:14], rc_send.at[it, 0], rc_recv.at[it, 0], partner)])

        if it == 0:
            when(has_down, lambda: edge_up(down).wait_recv())
            when(has_up, lambda: edge_down(up).wait_recv())
            for i in range(2):
                expo[i] = block_swap(exp_prev[8 * i : 8 * i + 8, :])
                expo[34 + i] = block_swap(exp_follow[8 * i : 8 * i + 8, :])
        when(has_down, lambda: pass_halo(it, 0).wait_recv())
        when(has_up, lambda: pass_halo(it, 1).wait_recv())
        for buf, at in ((prev, 0), (follow, 288)):
            value = buf[it].reshape(32, 256)
            mid[at : at + 32, :] = value
            put_near(value, at, near)
        blurred = product(mid, near, ((0, 4), (32, 4)), x_hi, x_lo, flip_hi, flip_lo)
        for low, source, count, weight, comes in (
            (0, 0, 2, w_down, has_down),
            (2, 16, 2, w_here, None),
            (32, 32, 2, w_here, None),
            (34, 48, 2, w_up, has_up),
        ):
            value = weight * expo[low : low + count].reshape(16, 256) / blurred[source : source + 16]
            if comes is not None:
                value = jnp.where(comes, value, 0.0)
            rmid[8 * low : 8 * low + 16, :] = value
            put_near(value, 8 * low, rnear)

        arrive(swap)
        a_sum[it, 2:14] = nums[it, 2:14, c] + r_core[it, 2:14]

        def owners(d):
            return ((z + d[0]) % 4) * 4 + (y + d[1]) % 4

        def at_edge(place):
            return (place < 2) | (place >= 14)

        spread = [
            remote(a_sum.at[it, owners(d)], r_in.at[it, i], rs_send.at[it, i], rs_recv.at[it, i], there(d))
            for i, d in enumerate(AWAY)
        ]
        for d, copy in zip(AWAY, spread):
            when(jnp.logical_not(at_edge(owners(d))), copy.start)

        found = product(rmid, rnear, ((0, 4), (28, 4)), x_hi, x_lo, fwd_hi, fwd_lo)
        nums[it, 0:2] = found[0:32].reshape(2, 2, 8, 256)
        nums[it, 14:16] = found[32:64].reshape(2, 2, 8, 256)
        swap = start(
            [
                remote(nums.at[it, at : at + 2, 1 - c], r_core.at[it, at : at + 2], rc_send.at[it, k], rc_recv.at[it, k], partner)
                for k, at in ((1, 0), (2, 14))
            ]
        )
        arrive(swap)
        for at in (0, 14):
            a_sum[it, at : at + 2] = nums[it, at : at + 2, c] + r_core[it, at : at + 2]
        for d, copy in zip(AWAY, spread):
            when(at_edge(owners(d)), copy.start)
        sent.extend(spread)

        if it == 0:
            arrive(q_spread)
            line = q_sum[u]
            for i in range(15):
                line = line + q_in[i]
            cover = iota((128, 256), 1) + iota((128, 256), 0) - 15
            valid = ((cover >= 0) & (cover < 256) & (iota((128, 256), 0) < 31)).astype(F32)
            norm = block_swap(jnp.dot(line, valid, precision=HI, preferred_element_type=F32))

        arrive(spread)
        total = a_sum[it, u]
        for i in range(15):
            total = total + r_in[it, i]
        model = own[it, u, c] * total / norm
        if it < ITERS - 1:
            own[it + 1, u, c] = model
        else:
            out_ref[...] = block_swap(model)

    for copy in sent:
        copy.wait_send()
    when(has_up, lambda: edge_up(up).wait_send())
    when(has_down, lambda: edge_down(down).wait_send())
    for it in range(ITERS):
        when(last & has_up, lambda: hop_up(it, up).wait_send())
        when(first & has_down, lambda: hop_down(it, down).wait_send())
        for which, comes, relayer in ((0, has_down, last), (1, has_up, first)):

            def drain(which=which):
                for copy in relay(it, which):
                    copy.wait_send()

            when(comes & relayer, drain)
            when(comes, lambda which=which: pass_halo(it, which).wait_send())


def body(exposures, sky_model, blur_kernels, coverage):
    vmem = pl.BlockSpec(memory_space=pltpu.VMEM)
    V = pltpu.VMEM
    D = pltpu.SemaphoreType.DMA
    op = V((7, 2, 8, 32, 256), BF)
    return pl.pallas_call(
        kernel,
        out_shape=jax.ShapeDtypeStruct((8, 256), F32),
        in_specs=[pl.BlockSpec(memory_space=pl.ANY), vmem, vmem, pl.BlockSpec(memory_space=pltpu.SMEM)],
        out_specs=vmem,
        scratch_shapes=[
            V((256, 256), F32), V((32, 128), F32), V((48, 128), F32), op, op, op, op,
            V((320, 256), F32), V((320, 256), F32), V((288, 256), F32), V((288, 256), F32),
            V((224, 2560), BF), V((224, 2560), BF),
            V((2, 16, 2, 8, 256), F32), V((2, 2, 2, 8, 256), F32), V((2, 2, 2, 8, 256), F32),
            V((16, 256), F32), V((16, 256), F32), V((36, 8, 256), F32),
            V((16, 2, 8, 128), F32), V((16, 8, 128), F32), V((16, 8, 128), F32), V((15, 8, 128), F32),
            V((2, 16, 2, 8, 256), F32), V((2, 16, 8, 256), F32), V((2, 16, 8, 256), F32), V((2, 15, 8, 256), F32),
            D, D((2, 15)), D((2, 15)), D((2, 4)), D((2, 4)), D((2, 2)), D((2, 2)), D((2, 2, 15)), D((2, 2, 2)),
            D((2, 2)), D((2, 2)), D((2, 3)), D((2, 3)), D((2, 15)), D((2, 15)), D((16,)), D((16,)), D((2,)), D((2,)),
        ],
        compiler_params=pltpu.CompilerParams(collective_id=0, has_side_effects=True),
    )(exposures, sky_model, jnp.transpose(blur_kernels, (1, 0, 2)), coverage)


def solution(mesh):
    return jax.shard_map(
        body,
        mesh=mesh,
        in_specs=(
            P("visit", "tile", None),
            P(("tile", "visit"), None),
            P("visit", None, None),
            P("visit", None),
        ),
        out_specs=P(("tile", "visit"), None),
        check_vma=False,
    )
```

```python
import jax
import jax.numpy as jnp
from jax import lax
from jax.experimental import pallas as pl
from jax.experimental.pallas import tpu as pltpu
from jax.sharding import PartitionSpec as P

F32 = jnp.float32
BF = jnp.bfloat16
HI = lax.Precision.HIGHEST
MESH = pl.DeviceIdType.MESH
ITERS = 2


def iota(shape, dim):
    return lax.broadcasted_iota(jnp.int32, shape, dim)


def block_swap(x):
    s = iota((8, 256), 0)
    b = iota((8, 256), 1) // 32
    out = x
    for d in range(1, 8):
        moved = pltpu.roll(pltpu.roll(x, d, 0), 256 - 32 * d, 1)
        out = jnp.where((s - b) % 8 == d, moved, out)
    return out


def build_rows(k, rows):
    rows[...] = jnp.zeros_like(rows)
    m = iota((128, 128), 1)
    b = iota((128, 128), 0)
    for r in range(4):
        pick = ((m == (32 * r - 1 - b + 256) % 128) & (b < 31)).astype(F32)
        moved = jnp.dot(k, pick, precision=HI, preferred_element_type=F32)
        rows[5 + r : 37 + r, :] = rows[5 + r : 37 + r, :] + moved


def build_operator(rows, op_hi, op_lo):
    c2 = iota((64, 128), 0)
    b = c2 - 1 - iota((64, 128), 1) % 32
    inside = (b >= 0) & (b <= 30)

    def step(j, carry):
        wide = jnp.broadcast_to(rows[pl.ds(j, 1), :], (8, 128))
        base = pltpu.roll(wide, 0, 1, stride=1, stride_axis=0)
        value = jnp.concatenate([base] + [pltpu.roll(base, 8 * i, 1) for i in range(1, 8)], axis=0)
        value = jnp.where(inside, value, 0.0)
        hi = value.astype(BF)
        lo = (value - hi.astype(F32)).astype(BF)
        for shift, lanes in ((4, slice(0, 128)), (8, slice(128, 256))):
            o, r = (j + shift) // 8, (j + shift) % 8
            for op, x in ((op_hi, hi), (op_lo, lo)):
                op[o, 0, r, :, lanes] = x[16:48]
                op[o, 1, r, 0:16, lanes] = x[48:64]
                op[o, 1, r, 16:32, lanes] = x[0:16]
        return carry

    lax.fori_loop(0, 44, step, 0, unroll=11)


def beside(value):
    n = value.shape[0]
    group = iota(value.shape, 0) % 8
    before = jnp.where(group > 0, pltpu.roll(value, 1, 0), 0.0)
    after = jnp.where(group < 7, pltpu.roll(value, n - 1, 0), 0.0)
    return jnp.where(iota(value.shape, 1) % 32 < 16, after, before)


def put(value, first, mid, near):
    n = value.shape[0]
    mid[first : first + n, :] = value
    near[first : first + n, :] = beside(value)


def weave(ref, first, count):
    pairs = [ref[0, first : first + count], ref[1, first : first + count]]
    return jnp.stack(pairs, axis=1).reshape(16 * count, 256)


def encode(value, code, rows, lanes):
    hi = value.astype(BF)
    code[0, rows, lanes] = hi
    code[1, rows, lanes] = (value - hi.astype(F32)).astype(BF)


def encode_rows(mid, near, code, shift, first, last):
    for at in range(first, last, 64):
        n = min(64, last - at)
        for k, src in ((0, mid), (1, near)):
            rows = slice(at + 8 * shift, at + 8 * shift + n)
            encode(src[rows, :], code.at[shift], slice(at, at + n), slice(256 * k, 256 * k + 256))


def multiply(left, op_hi, op_lo):
    def dot(x, op):
        return jnp.dot(x, op[1:6].reshape(2560, 256), preferred_element_type=F32)

    hi, lo = left
    return dot(hi, op_hi) + (dot(hi, op_lo) + dot(lo, op_hi))


def product(code, ranges, op_hi, op_lo):
    left = []
    for term in range(2):
        parts = []
        for first, count in ranges:
            at = [8 * first + 16 * (o // 2) for o in range(5)]
            parts.append(
                jnp.concatenate([code[o % 2, term, at[o] : at[o] + 8 * count, :] for o in range(5)], axis=1)
            )
        left.append(jnp.concatenate(parts, axis=0) if len(parts) > 1 else parts[0])
    return multiply(left, op_hi, op_lo)


def product_half(code, parity, op_hi, op_lo):
    left = []
    for term in range(2):
        parts = []
        for o in range(5):
            pair = (parity + o) // 2
            at = pl.multiple_of((pair // 2) * 16, 16)
            parts.append(code[(parity + o) % 2, pair % 2, term, pl.ds(at, 128), :])
        left.append(jnp.concatenate(parts, axis=1))
    return multiply(left, op_hi, op_lo)


def far(d):
    return -(d[0] + (2 if d[1] == 2 else 1 if d[1] else 0))


AWAY = sorted([(dz, dy) for dz in range(4) for dy in range(4) if (dz, dy) != (0, 0)], key=far)
SENDS = ("ag1", "hand1", "qswap", "qsum", "qx", "swap1", "swap2", "rs1", "x", "ag2", "hand2", "xg", "swap3", "rs2")
SENDS += ("hop0", "hop1", "relay0", "relay1", "pass0", "pass1", "edge0", "edge1")
ARRIVALS = SENDS + ("ag1_1", "ag1_2", "ag1_3", "ag2_1", "ag2_2", "ag2_3")


def is_extra(u):
    return (u == 5) | (u == 6) | (u == 9) | (u == 10)


def extra_pair(u):
    return jnp.where(u < 8, u - 5, u + 9)


def kernel(
    exp_hbm, sky_ref, ker_ref, cov_ref, out_ref,
    exp_ref, kpad, rows, fwd_hi, fwd_lo, flip_hi, flip_lo, mid, near, rmid, rnear, hmid, hnear, code, rcode, hcode,
    own, prev, follow, model, exp_prev, exp_follow, expo, norms,
    q_all, q_core, q_sum, q_in, qx_in, nums, r_core, a_sum, r_in, x_in, nums2, r_core2, a_sum2, r_in2,
    exp_sem, send_sems, recv_sems,
):
    t = lax.axis_index("tile")
    v = lax.axis_index("visit")
    tiles = lax.axis_size("tile")
    z, y, c = v // 8, (v // 2) % 4, v % 2
    u = v // 2

    def chip(d):
        return ((z + d[0]) % 4) * 4 + (y + d[1]) % 4

    def there(d):
        return {"visit": 2 * chip(d) + c, "tile": t}

    partner = {"visit": 2 * u + (1 - c), "tile": t}
    up = {"visit": v, "tile": t + 1}
    down = {"visit": v, "tile": t - 1}
    has_up = t < tiles - 1
    has_down = t > 0
    extra = is_extra(u)

    prev[...] = jnp.zeros_like(prev)
    follow[...] = jnp.zeros_like(follow)
    barrier = pltpu.get_barrier_semaphore()
    for peer in [there(d) for d in AWAY] + [partner]:
        pl.semaphore_signal(barrier, inc=1, device_id=peer, device_id_type=MESH)

    @pl.when(has_up)
    def _():
        pl.semaphore_signal(barrier, inc=1, device_id=up, device_id_type=MESH)

    @pl.when(has_down)
    def _():
        pl.semaphore_signal(barrier, inc=1, device_id=down, device_id_type=MESH)

    load = pltpu.make_async_copy(exp_hbm.at[0], exp_ref, exp_sem)
    load.start()

    def remote(src, dst, name, device, arrival=None):
        return pltpu.make_async_remote_copy(
            src_ref=src,
            dst_ref=dst,
            send_sem=send_sems.at[SENDS.index(name)],
            recv_sem=recv_sems.at[ARRIVALS.index(arrival or name)],
            device_id=device,
            device_id_type=MESH,
        )

    def got(ref, name):
        remote(ref, ref, "ag1", partner, name).wait_recv()

    def gone(ref, name):
        remote(ref, ref, name, partner).wait_send()

    def when(cond, act):
        pl.when(cond)(act)

    own[c, u] = block_swap(sky_ref[...])
    kpad[...] = jnp.zeros_like(kpad)
    raw = ker_ref[:, 0, :]
    kpad[0:31, 0:31] = raw / jnp.sum(raw)
    w_here = cov_ref[0, t].astype(F32)
    w_down = jnp.where(has_down, cov_ref[0, jnp.maximum(t - 1, 0)], 0).astype(F32)
    w_up = jnp.where(has_up, cov_ref[0, jnp.minimum(t + 1, tiles - 1)], 0).astype(F32)
    i128, a32 = iota((128, 32), 0), iota((128, 32), 1)
    weights = jnp.where(
        i128 < 64,
        jnp.where(i128 + a32 < 47, w_down, w_here),
        jnp.where(i128 + a32 >= 111, w_up, w_here),
    )
    lines = jnp.dot(weights, kpad[...], precision=HI, preferred_element_type=F32)
    for b in range(40):
        at = 8 * b if b < 8 else 64 + 8 * (b - 32) if b >= 32 else 48
        q_all[b % 2, b // 2] = lines[at : at + 8]
    turn_rows = (iota((32, 32), 0) + iota((32, 32), 1) == 30).astype(F32)
    turn_cols = (iota((128, 128), 0) + iota((128, 128), 1) == 30).astype(F32)
    turned = jnp.dot(turn_rows, kpad[...], precision=HI, preferred_element_type=F32)
    turned = jnp.dot(turned, turn_cols, precision=HI, preferred_element_type=F32)
    build_rows(turned, rows)
    build_operator(rows, flip_hi, flip_lo)

    pl.semaphore_wait(barrier, 16 + has_up.astype(jnp.int32) + has_down.astype(jnp.int32))

    edge_up = remote(exp_ref.at[208:256, :], exp_prev, "edge0", up)
    edge_down = remote(exp_ref.at[0:48, :], exp_follow, "edge1", down)
    mine = own.at[c, u]
    hop_up = remote(mine, prev.at[c, u % 4], "hop0", up)
    hop_down = remote(mine, follow.at[c, u % 4], "hop1", down)
    last = u >= 12
    first = u < 4

    def relay_up():
        got(prev.at[c, u % 4], "hop0")
        block = prev.at[c, u % 4]
        for d in AWAY:
            remote(block, block, "relay0", there(d)).start()

    def relay_down():
        got(follow.at[c, u % 4], "hop1")
        block = follow.at[c, u % 4]
        for d in AWAY:
            remote(block, block, "relay1", there(d)).start()

    def hand_over(halo, name, relayed, comes, relayer):
        when(comes & relayer, lambda: got(halo.at[c, 0:3], relayed))
        when(comes & jnp.logical_not(relayer), lambda: got(halo.at[c], relayed))
        when(comes, lambda: remote(halo.at[c], halo.at[c], name, partner).start())

    when(last & has_up, hop_up.start)
    when(first & has_down, hop_down.start)
    for d in AWAY:
        remote(mine, mine, "ag1", there(d), ("ag1", "ag1_1", "ag1_2", "ag1_3")[d[0]]).start()
    remote(q_all.at[1 - c], q_core, "qswap", partner).start()
    load.wait()
    when(has_up, edge_up.start)
    when(has_down, edge_down.start)
    build_rows(kpad[...], rows)
    build_operator(rows, fwd_hi, fwd_lo)
    when(last & has_down, relay_up)
    when(first & has_up, relay_down)

    def swap_exposure(i, carry):
        for j in range(4):
            at = pl.multiple_of(32 * i + 8 * j, 8)
            expo[4 * i + j + 6] = block_swap(exp_ref[pl.ds(at, 8), :])
        return carry

    lax.fori_loop(0, 8, swap_exposure, 0)

    for dz, name in enumerate(("ag1", "ag1_1", "ag1_2", "ag1_3")):
        got(own.at[c, 0 : 4 if dz else 3], name)
        part = own.at[c, pl.ds(((z - dz) % 4) * 4, 4)]
        remote(part, part, "hand1", partner).start()
    got(q_core, "qswap")
    q_sum[...] = q_all[c] + q_core[...]
    for i, d in enumerate(AWAY):
        remote(q_sum.at[chip(d) + 2], q_in.at[i], "qsum", there(d)).start()
    for i, d in enumerate(AWAY):
        when(is_extra(chip(d)), remote(q_sum.at[extra_pair(chip(d))], qx_in.at[i], "qx", there(d)).start)
    got(own.at[c], "hand1")

    for g in range(4):
        put(weave(own, 4 * g, 4), 64 + 64 * g, mid, near)
    encode_rows(mid, near, code, 0, 64, 320)
    encode_rows(mid, near, code, 1, 64, 304)
    blurred = product(code, ((8, 28),), flip_hi, flip_lo)
    value = w_here * expo[8:36].reshape(224, 256) / blurred
    for g in range(7):
        put(value[32 * g : 32 * g + 32], 64 + 32 * g, rmid, rnear)
    encode_rows(rmid, rnear, rcode, 0, 64, 288)
    encode_rows(rmid, rnear, rcode, 1, 64, 272)

    far_prev = t == tiles // 2
    far_follow = t == tiles // 2 - 1
    hand_over(prev, "pass0", "relay0", has_down & jnp.logical_not(far_prev), last)
    hand_over(follow, "pass1", "relay1", has_up & jnp.logical_not(far_follow), first)
    found = product(rcode, ((8, 24),), fwd_hi, fwd_lo).reshape(12, 2, 8, 256)
    for k in range(2):
        nums[k, 4:16] = found[:, k]
    remote(nums.at[1 - c, 4:16], r_core.at[4:16], "swap1", partner).start()
    hand_over(prev, "pass0", "relay0", far_prev, last)
    hand_over(follow, "pass1", "relay1", far_follow, first)

    when(has_down, lambda: got(exp_prev, "edge0"))
    when(has_up, lambda: got(exp_follow, "edge1"))

    def swap_edges(i, carry):
        at = pl.multiple_of(8 * i, 8)
        expo[i] = block_swap(exp_prev[pl.ds(at, 8), :])
        expo[38 + i] = block_swap(exp_follow[pl.ds(at, 8), :])
        return carry

    lax.fori_loop(0, 6, swap_edges, 0, unroll=2)
    got(r_core.at[4:16], "swap1")
    a_sum[4:16] = nums[c, 4:16] + r_core[4:16]

    def at_edge(place):
        return (place < 2) | (place >= 14)

    spread = [remote(a_sum.at[chip(d) + 2], r_in.at[i], "rs1", there(d)) for i, d in enumerate(AWAY)]
    x_spread = [remote(a_sum.at[extra_pair(chip(d))], x_in.at[i], "x", there(d)) for i, d in enumerate(AWAY)]
    for d, copy in zip(AWAY, spread):
        when(jnp.logical_not(at_edge(chip(d))), copy.start)

    when(has_down, lambda: got(prev.at[1 - c], "pass0"))
    when(has_up, lambda: got(follow.at[1 - c], "pass1"))
    put(weave(prev, 0, 4), 0, mid, near)
    put(weave(follow, 0, 4), 320, mid, near)
    encode_rows(mid, near, code, 0, 0, 64)
    encode_rows(mid, near, code, 1, 0, 64)
    encode_rows(mid, near, code, 0, 320, 384)
    encode_rows(mid, near, code, 1, 304, 368)
    blurred = product(code, ((0, 8), (36, 8)), flip_hi, flip_lo)
    for low, source, count, weight, comes in (
        (0, 0, 6, w_down, has_down),
        (6, 48, 2, w_here, None),
        (36, 64, 2, w_here, None),
        (38, 80, 6, w_up, has_up),
    ):
        m = 8 * count
        value = weight * expo[low : low + count].reshape(m, 256) / blurred[source : source + m]
        if comes is not None:
            value = jnp.where(comes, value, 0.0)
        put(value, 8 * low, rmid, rnear)
    encode_rows(rmid, rnear, rcode, 0, 0, 64)
    encode_rows(rmid, rnear, rcode, 1, 0, 64)
    encode_rows(rmid, rnear, rcode, 0, 288, 352)
    encode_rows(rmid, rnear, rcode, 1, 272, 336)
    found = product(rcode, ((0, 8), (32, 8)), fwd_hi, fwd_lo).reshape(8, 2, 8, 256)
    for k in range(2):
        nums[k, 0:4] = found[0:4, k]
        nums[k, 16:20] = found[4:8, k]
    for at in (0, 16):
        remote(nums.at[1 - c, at : at + 4], r_core.at[at : at + 4], "swap2", partner).start()

    def normal(line):
        cover = iota((128, 256), 1) + iota((128, 256), 0) - 15
        valid = ((cover >= 0) & (cover < 256) & (iota((128, 256), 0) < 31)).astype(F32)
        return block_swap(jnp.dot(line, valid, precision=HI, preferred_element_type=F32))

    def total_of(own_part, parts):
        total = own_part
        for i in range(15):
            total = total + parts[i]
        return total

    got(q_in, "qsum")
    norm = normal(total_of(q_sum[u + 2], q_in))
    pair = jnp.where(extra, extra_pair(u), 0)

    @pl.when(extra)
    def _():
        got(qx_in, "qx")
        norms[...] = normal(total_of(q_sum[pair], qx_in))

    got(r_core.at[0:8], "swap2")
    for at in (0, 16):
        a_sum[at : at + 4] = nums[c, at : at + 4] + r_core[at : at + 4]
    for d, copy, x_copy in zip(AWAY, spread, x_spread):
        when(at_edge(chip(d)), copy.start)
        when(is_extra(chip(d)), x_copy.start)

    got(r_in, "rs1")
    model[c, u + 2] = own[c, u] * total_of(a_sum[u + 2], r_in) / norm

    mine = model.at[c, u + 2]
    for d in AWAY:
        remote(mine, mine, "ag2", there(d), ("ag2", "ag2_1", "ag2_2", "ag2_3")[d[0]]).start()

    @pl.when(extra)
    def _():
        got(x_in, "x")
        before = prev[c, jnp.where(u < 8, u - 3, 2)]
        after = follow[c, jnp.where(u < 8, 0, u - 9)]
        exists = jnp.where(u < 8, has_down.astype(jnp.int32), has_up.astype(jnp.int32)) > 0
        old = jnp.where(u < 8, before, after)
        new = old * total_of(a_sum[pair], x_in) / norms[...]
        model[c, pair] = jnp.where(exists, new, 0.0)
        block = model.at[c, pair]
        for d in AWAY:
            remote(block, block, "xg", there(d)).start()

    for dz, name in enumerate(("ag2", "ag2_1", "ag2_2", "ag2_3")):
        got(model.at[c, 0 : 4 if dz else 3], name)
        part = model.at[c, pl.ds(((z - dz) % 4) * 4 + 2, 4)]
        remote(part, part, "hand2", partner).start()
    when(extra, lambda: got(model.at[c, 0:3], "xg"))
    when(jnp.logical_not(extra), lambda: got(model.at[c, 0:4], "xg"))
    for at in (0, 18):
        part = model.at[c, at : at + 2]
        remote(part, part, "hand2", partner).start()
    got(model.at[c], "hand2")

    for g in range(5):
        put(weave(model, 4 * g, 4), 64 * g, mid, near)
    encode_rows(mid, near, code, 0, 0, 320)
    encode_rows(mid, near, code, 1, 0, 304)
    blurred = product(code, ((0, 36),), flip_hi, flip_lo)
    for low, count, weight, comes in ((0, 2, w_down, has_down), (2, 32, w_here, None), (34, 2, w_up, has_up)):
        for g in range(low, low + count, 4):
            n = min(4, low + count - g)
            value = weight * expo[g + 4 : g + 4 + n].reshape(8 * n, 256) / blurred[8 * g : 8 * g + 8 * n]
            if comes is not None:
                value = jnp.where(comes, value, 0.0)
            hmid[g // 2 : (g + n) // 2] = value.reshape(n // 2, 2, 8, 256)
            hnear[g // 2 : (g + n) // 2] = beside(value).reshape(n // 2, 2, 8, 256)
    for parity in range(2):
        for shift, count in ((0, 18), (1, 16)):
            for k, src in ((0, hmid), (1, hnear)):
                value = src[shift : shift + count, parity].reshape(8 * count, 256)
                lanes = slice(256 * k, 256 * k + 256)
                encode(value, hcode.at[parity, shift], slice(0, 8 * count), lanes)
    nums2[0] = product_half(hcode, 1 - c, fwd_hi, fwd_lo).reshape(16, 8, 256)
    remote(nums2.at[0], r_core2, "swap3", partner).start()
    nums2[1] = product_half(hcode, c, fwd_hi, fwd_lo).reshape(16, 8, 256)
    got(r_core2, "swap3")
    a_sum2[...] = nums2[1] + r_core2[...]
    for i, d in enumerate(AWAY):
        remote(a_sum2.at[chip(d)], r_in2.at[i], "rs2", there(d)).start()
    got(r_in2, "rs2")
    out_ref[...] = block_swap(model[c, u + 2] * total_of(a_sum2[u], r_in2) / norm)

    for name in ("ag1", "rs1", "ag2", "rs2"):
        gone(r_in, name)
    gone(own.at[c], "hand1")
    gone(q_core, "qswap")
    gone(q_in, "qsum")
    gone(r_core.at[4:16], "swap1")
    gone(r_core.at[0:8], "swap2")
    gone(model.at[c], "hand2")
    gone(r_core2, "swap3")
    for ref, name in ((q_in, "qx"), (x_in, "x")):
        when(extra, lambda ref=ref, name=name: gone(ref.at[0:3], name))
        when(jnp.logical_not(extra), lambda ref=ref, name=name: gone(ref.at[0:4], name))
    when(extra, lambda: gone(x_in, "xg"))
    when(has_up, lambda: gone(exp_prev, "edge0"))
    when(has_down, lambda: gone(exp_follow, "edge1"))
    when(last & has_up, lambda: gone(prev.at[c, 0], "hop0"))
    when(first & has_down, lambda: gone(prev.at[c, 0], "hop1"))
    when(last & has_down, lambda: gone(x_in, "relay0"))
    when(first & has_up, lambda: gone(x_in, "relay1"))
    when(has_down, lambda: gone(prev.at[c], "pass0"))
    when(has_up, lambda: gone(prev.at[c], "pass1"))


def body(exposures, sky_model, blur_kernels, coverage):
    vmem = pl.BlockSpec(memory_space=pltpu.VMEM)
    V = pltpu.VMEM
    D = pltpu.SemaphoreType.DMA
    op = V((7, 2, 8, 32, 256), BF)

    def blocks(*dims):
        return V((*dims, 8, 256), F32)

    def lanes(*dims):
        return V((*dims, 8, 128), F32)

    return pl.pallas_call(
        kernel,
        out_shape=jax.ShapeDtypeStruct((8, 256), F32),
        in_specs=[pl.BlockSpec(memory_space=pl.ANY), vmem, vmem, pl.BlockSpec(memory_space=pltpu.SMEM)],
        out_specs=vmem,
        scratch_shapes=[
            V((256, 256), F32), V((32, 128), F32), V((48, 128), F32), op, op, op, op,
            V((384, 256), F32), V((384, 256), F32), V((352, 256), F32), V((352, 256), F32),
            blocks(18, 2), blocks(18, 2), V((2, 2, 384, 512), BF), V((2, 2, 352, 512), BF), V((2, 2, 2, 144, 512), BF),
            blocks(2, 16), blocks(2, 4), blocks(2, 4), blocks(2, 20), V((48, 256), F32), V((48, 256), F32), blocks(44),
            V((8, 256), F32),
            lanes(2, 20), lanes(20), lanes(20), lanes(15), lanes(15),
            blocks(2, 20), blocks(20), blocks(20), blocks(15), blocks(15), blocks(2, 16), blocks(16), blocks(16), blocks(15),
            D, D((len(SENDS),)), D((len(ARRIVALS),)),
        ],
        compiler_params=pltpu.CompilerParams(collective_id=0, has_side_effects=True),
    )(exposures, sky_model, jnp.transpose(blur_kernels, (1, 0, 2)), coverage)


def solution(mesh):
    return jax.shard_map(
        body,
        mesh=mesh,
        in_specs=(
            P("visit", "tile", None),
            P(("tile", "visit"), None),
            P("visit", None, None),
            P("visit", None),
        ),
        out_specs=P(("tile", "visit"), None),
        check_vma=False,
    )
```

```python
import jax
import jax.numpy as jnp
from jax import lax
from jax.experimental import pallas as pl
from jax.experimental.pallas import tpu as pltpu
from jax.sharding import PartitionSpec as P

F32 = jnp.float32
BF = jnp.bfloat16
HI = lax.Precision.HIGHEST
MESH = pl.DeviceIdType.MESH
ITERS = 2


def iota(shape, dim):
    return lax.broadcasted_iota(jnp.int32, shape, dim)


def block_swap(x):
    s = iota((8, 256), 0)
    b = iota((8, 256), 1) // 32
    out = x
    for d in range(1, 8):
        moved = pltpu.roll(pltpu.roll(x, d, 0), 256 - 32 * d, 1)
        out = jnp.where((s - b) % 8 == d, moved, out)
    return out


def build_rows(k, rows):
    rows[...] = jnp.zeros_like(rows)
    m = iota((128, 128), 1)
    b = iota((128, 128), 0)
    for r in range(4):
        pick = ((m == (32 * r - 1 - b + 256) % 128) & (b < 31)).astype(F32)
        moved = jnp.dot(k, pick, precision=HI, preferred_element_type=F32)
        rows[5 + r : 37 + r, :] = rows[5 + r : 37 + r, :] + moved


def build_operator(rows, op_hi, op_lo):
    c2 = iota((64, 128), 0)
    b = c2 - 1 - iota((64, 128), 1) % 32
    inside = (b >= 0) & (b <= 30)

    def step(j, carry):
        wide = jnp.broadcast_to(rows[pl.ds(j, 1), :], (8, 128))
        base = pltpu.roll(wide, 0, 1, stride=1, stride_axis=0)
        value = jnp.concatenate([base] + [pltpu.roll(base, 8 * i, 1) for i in range(1, 8)], axis=0)
        value = jnp.where(inside, value, 0.0)
        hi = value.astype(BF)
        lo = (value - hi.astype(F32)).astype(BF)
        for shift, lanes in ((4, slice(0, 128)), (8, slice(128, 256))):
            o, r = (j + shift) // 8, (j + shift) % 8
            for op, x in ((op_hi, hi), (op_lo, lo)):
                op[o, 0, r, :, lanes] = x[16:48]
                op[o, 1, r, 0:16, lanes] = x[48:64]
                op[o, 1, r, 16:32, lanes] = x[0:16]
        return carry

    lax.fori_loop(0, 44, step, 0, unroll=11)


def beside(value):
    n = value.shape[0]
    group = iota(value.shape, 0) % 8
    before = jnp.where(group > 0, pltpu.roll(value, 1, 0), 0.0)
    after = jnp.where(group < 7, pltpu.roll(value, n - 1, 0), 0.0)
    return jnp.where(iota(value.shape, 1) % 32 < 16, after, before)


def put(value, first, mid, near):
    n = value.shape[0]
    mid[first : first + n, :] = value
    near[first : first + n, :] = beside(value)


def weave(ref, first, count):
    pairs = [ref[0, first : first + count], ref[1, first : first + count]]
    return jnp.stack(pairs, axis=1).reshape(16 * count, 256)


def encode(value, code, rows, lanes):
    hi = value.astype(BF)
    code[0, rows, lanes] = hi
    code[1, rows, lanes] = (value - hi.astype(F32)).astype(BF)


def encode_rows(mid, near, code, shift, first, last):
    for at in range(first, last, 64):
        n = min(64, last - at)
        for k, src in ((0, mid), (1, near)):
            rows = slice(at + 8 * shift, at + 8 * shift + n)
            encode(src[rows, :], code.at[shift], slice(at, at + n), slice(256 * k, 256 * k + 256))


def multiply(left, op_hi, op_lo):
    def dot(x, op):
        return jnp.dot(x, op[1:6].reshape(2560, 256), preferred_element_type=F32)

    hi, lo = left
    return dot(hi, op_hi) + (dot(hi, op_lo) + dot(lo, op_hi))


def product(code, ranges, op_hi, op_lo):
    left = []
    for term in range(2):
        parts = []
        for first, count in ranges:
            at = [8 * first + 16 * (o // 2) for o in range(5)]
            parts.append(
                jnp.concatenate([code[o % 2, term, at[o] : at[o] + 8 * count, :] for o in range(5)], axis=1)
            )
        left.append(jnp.concatenate(parts, axis=0) if len(parts) > 1 else parts[0])
    return multiply(left, op_hi, op_lo)


def product_half(code, parity, op_hi, op_lo):
    left = []
    for term in range(2):
        parts = []
        for o in range(5):
            pair = (parity + o) // 2
            at = pl.multiple_of((pair // 2) * 16, 16)
            parts.append(code[(parity + o) % 2, pair % 2, term, pl.ds(at, 128), :])
        left.append(jnp.concatenate(parts, axis=1))
    return multiply(left, op_hi, op_lo)


def far(d):
    return -(d[0] + (2 if d[1] == 2 else 1 if d[1] else 0))


AWAY = sorted([(dz, dy) for dz in range(4) for dy in range(4) if (dz, dy) != (0, 0)], key=far)
SENDS = ("ag1", "hand1", "qswap", "qsum", "qx", "swap1", "swap2", "rs1", "x", "ag2", "hand2", "xg", "swap3", "rs2")
SENDS += ("hop0", "hop1", "relay0", "relay1", "pass0", "pass1", "edge0", "edge1")
ARRIVALS = ("ag1_0", "ag1_1", "ag1_2", "ag1_3", "ag2_0", "ag2_1", "ag2_2", "ag2_3") + SENDS


def is_extra(u):
    return (u == 5) | (u == 6) | (u == 9) | (u == 10)


def extra_pair(u):
    return jnp.where(u < 8, u - 5, u + 9)


def kernel(
    exp_hbm, sky_hbm, ker_hbm, cov_hbm, out_ref,
    exp_ref, sky_ref, ker_ref, cov_ref, kpad, rows, fwd_hi, fwd_lo, flip_hi, flip_lo, mid, near, rmid, rnear, hmid, hnear, code, rcode, hcode,
    own, prev, follow, model, exp_prev, exp_follow, expo, norms,
    q_all, q_core, q_sum, q_in, qx_in, nums, r_core, a_sum, r_in, x_in, nums2, r_core2, a_sum2, r_in2,
    load_sems, send_sems, recv_sems,
):
    t = lax.axis_index("tile")
    v = lax.axis_index("visit")
    tiles = lax.axis_size("tile")
    z, y, c = v // 8, (v // 2) % 4, v % 2
    u = v // 2

    def chip(d):
        return ((z + d[0]) % 4) * 4 + (y + d[1]) % 4

    def there(d):
        return {"visit": 2 * chip(d) + c, "tile": t}

    partner = {"visit": 2 * u + (1 - c), "tile": t}
    up = {"visit": v, "tile": t + 1}
    down = {"visit": v, "tile": t - 1}
    has_up = t < tiles - 1
    has_down = t > 0
    extra = is_extra(u)

    loads = [
        pltpu.make_async_copy(src, dst, load_sems.at[i])
        for i, (src, dst) in enumerate(
            ((ker_hbm, ker_ref), (cov_hbm, cov_ref), (sky_hbm, sky_ref), (exp_hbm.at[0], exp_ref))
        )
    ]
    for copy in loads:
        copy.start()
    prev[...] = jnp.zeros_like(prev)
    follow[...] = jnp.zeros_like(follow)
    barrier = pltpu.get_barrier_semaphore()
    for peer in [there(d) for d in AWAY] + [partner]:
        pl.semaphore_signal(barrier, inc=1, device_id=peer, device_id_type=MESH)

    @pl.when(has_up)
    def _():
        pl.semaphore_signal(barrier, inc=1, device_id=up, device_id_type=MESH)

    @pl.when(has_down)
    def _():
        pl.semaphore_signal(barrier, inc=1, device_id=down, device_id_type=MESH)

    def remote(src, dst, name, device, arrival=None):
        return pltpu.make_async_remote_copy(
            src_ref=src,
            dst_ref=dst,
            send_sem=send_sems.at[SENDS.index(name)],
            recv_sem=recv_sems.at[ARRIVALS.index(name) if arrival is None else arrival],
            device_id=device,
            device_id_type=MESH,
        )

    def got(ref, name):
        remote(ref, ref, "ag1", partner, ARRIVALS.index(name)).wait_recv()

    def gone(ref, name):
        remote(ref, ref, name, partner).wait_send()

    def when(cond, act):
        pl.when(cond)(act)

    kpad[...] = jnp.zeros_like(kpad)
    loads[0].wait()
    raw = ker_ref[:, 0, :]
    kpad[0:31, 0:31] = raw / jnp.sum(raw)
    loads[1].wait()
    w_here = cov_ref[0, t].astype(F32)
    w_down = jnp.where(has_down, cov_ref[0, jnp.maximum(t - 1, 0)], 0).astype(F32)
    w_up = jnp.where(has_up, cov_ref[0, jnp.minimum(t + 1, tiles - 1)], 0).astype(F32)
    i128, a32 = iota((128, 32), 0), iota((128, 32), 1)
    weights = jnp.where(
        i128 < 64,
        jnp.where(i128 + a32 < 47, w_down, w_here),
        jnp.where(i128 + a32 >= 111, w_up, w_here),
    )
    lines = jnp.dot(weights, kpad[...], precision=HI, preferred_element_type=F32)
    for b in range(40):
        at = 8 * b if b < 8 else 64 + 8 * (b - 32) if b >= 32 else 48
        q_all[b % 2, b // 2] = lines[at : at + 8]
    loads[2].wait()
    own[c, u] = block_swap(sky_ref[...])
    turn_rows = (iota((32, 32), 0) + iota((32, 32), 1) == 30).astype(F32)
    turn_cols = (iota((128, 128), 0) + iota((128, 128), 1) == 30).astype(F32)
    turned = jnp.dot(turn_rows, kpad[...], precision=HI, preferred_element_type=F32)
    turned = jnp.dot(turned, turn_cols, precision=HI, preferred_element_type=F32)
    build_rows(turned, rows)
    build_operator(rows, flip_hi, flip_lo)

    pl.semaphore_wait(barrier, 16 + has_up.astype(jnp.int32) + has_down.astype(jnp.int32))

    edge_up = remote(exp_ref.at[208:256, :], exp_prev, "edge0", up)
    edge_down = remote(exp_ref.at[0:48, :], exp_follow, "edge1", down)
    mine = own.at[c, u]
    hop_up = remote(mine, prev.at[c, u % 4], "hop0", up)
    hop_down = remote(mine, follow.at[c, u % 4], "hop1", down)
    last = u >= 12
    first = u < 4

    def relay_up():
        got(prev.at[c, u % 4], "hop0")
        block = prev.at[c, u % 4]
        for d in AWAY:
            remote(block, block, "relay0", there(d)).start()

    def relay_down():
        got(follow.at[c, u % 4], "hop1")
        block = follow.at[c, u % 4]
        for d in AWAY:
            remote(block, block, "relay1", there(d)).start()

    def hand_over(halo, name, relayed, comes, relayer):
        when(comes & relayer, lambda: got(halo.at[c, 0:3], relayed))
        when(comes & jnp.logical_not(relayer), lambda: got(halo.at[c], relayed))
        when(comes, lambda: remote(halo.at[c], halo.at[c], name, partner).start())

    when(last & has_up, hop_up.start)
    when(first & has_down, hop_down.start)
    for d in AWAY:
        remote(mine, mine, "ag1", there(d), z).start()
    remote(q_all.at[1 - c], q_core, "qswap", partner).start()
    loads[3].wait()
    when(has_up, edge_up.start)
    when(has_down, edge_down.start)
    build_rows(kpad[...], rows)
    build_operator(rows, fwd_hi, fwd_lo)
    when(last & has_down, relay_up)
    when(first & has_up, relay_down)

    def swap_exposure(i, carry):
        for j in range(4):
            at = pl.multiple_of(32 * i + 8 * j, 8)
            expo[4 * i + j + 6] = block_swap(exp_ref[pl.ds(at, 8), :])
        return carry

    lax.fori_loop(0, 8, swap_exposure, 0)

    def got_row(ref, row, name):
        when(z == row, lambda: got(ref.at[c, 0:3], name))
        when(z != row, lambda: got(ref.at[c, 0:4], name))

    for row in (1, 2, 0, 3):
        got_row(own, row, "ag1_%d" % row)
        part = own.at[c, 4 * row : 4 * row + 4]
        remote(part, part, "hand1", partner).start()
    got(q_core, "qswap")
    q_sum[...] = q_all[c] + q_core[...]
    for i, d in enumerate(AWAY):
        remote(q_sum.at[chip(d) + 2], q_in.at[i], "qsum", there(d)).start()
    for i, d in enumerate(AWAY):
        when(is_extra(chip(d)), remote(q_sum.at[extra_pair(chip(d))], qx_in.at[i], "qx", there(d)).start)
    got(own.at[c], "hand1")

    for g in range(4):
        put(weave(own, 4 * g, 4), 64 + 64 * g, mid, near)
    encode_rows(mid, near, code, 0, 64, 320)
    encode_rows(mid, near, code, 1, 64, 304)
    blurred = product(code, ((8, 28),), flip_hi, flip_lo)
    value = w_here * expo[8:36].reshape(224, 256) / blurred
    for g in range(7):
        put(value[32 * g : 32 * g + 32], 64 + 32 * g, rmid, rnear)
    encode_rows(rmid, rnear, rcode, 0, 64, 288)
    encode_rows(rmid, rnear, rcode, 1, 64, 272)

    far_prev = t == tiles // 2
    far_follow = t == tiles // 2 - 1
    hand_over(prev, "pass0", "relay0", has_down & jnp.logical_not(far_prev), last)
    hand_over(follow, "pass1", "relay1", has_up & jnp.logical_not(far_follow), first)
    found = product(rcode, ((8, 24),), fwd_hi, fwd_lo).reshape(12, 2, 8, 256)
    for k in range(2):
        nums[k, 4:16] = found[:, k]
    remote(nums.at[1 - c, 4:16], r_core.at[4:16], "swap1", partner).start()
    hand_over(prev, "pass0", "relay0", far_prev, last)
    hand_over(follow, "pass1", "relay1", far_follow, first)

    when(has_down, lambda: got(exp_prev, "edge0"))
    when(has_up, lambda: got(exp_follow, "edge1"))

    def swap_edges(i, carry):
        at = pl.multiple_of(8 * i, 8)
        expo[i] = block_swap(exp_prev[pl.ds(at, 8), :])
        expo[38 + i] = block_swap(exp_follow[pl.ds(at, 8), :])
        return carry

    lax.fori_loop(0, 6, swap_edges, 0, unroll=2)
    got(r_core.at[4:16], "swap1")
    a_sum[4:16] = nums[c, 4:16] + r_core[4:16]

    def at_edge(place):
        return (place < 2) | (place >= 14)

    spread = [remote(a_sum.at[chip(d) + 2], r_in.at[i], "rs1", there(d)) for i, d in enumerate(AWAY)]
    x_spread = [remote(a_sum.at[extra_pair(chip(d))], x_in.at[i], "x", there(d)) for i, d in enumerate(AWAY)]
    for d, copy in zip(AWAY, spread):
        when(jnp.logical_not(at_edge(chip(d))), copy.start)

    when(has_down, lambda: got(prev.at[1 - c], "pass0"))
    when(has_up, lambda: got(follow.at[1 - c], "pass1"))
    put(weave(prev, 0, 4), 0, mid, near)
    put(weave(follow, 0, 4), 320, mid, near)
    encode_rows(mid, near, code, 0, 0, 64)
    encode_rows(mid, near, code, 1, 0, 64)
    encode_rows(mid, near, code, 0, 320, 384)
    encode_rows(mid, near, code, 1, 304, 368)
    blurred = product(code, ((0, 8), (36, 8)), flip_hi, flip_lo)
    for low, source, count, weight, comes in (
        (0, 0, 6, w_down, has_down),
        (6, 48, 2, w_here, None),
        (36, 64, 2, w_here, None),
        (38, 80, 6, w_up, has_up),
    ):
        m = 8 * count
        value = weight * expo[low : low + count].reshape(m, 256) / blurred[source : source + m]
        if comes is not None:
            value = jnp.where(comes, value, 0.0)
        put(value, 8 * low, rmid, rnear)
    encode_rows(rmid, rnear, rcode, 0, 0, 64)
    encode_rows(rmid, rnear, rcode, 1, 0, 64)
    encode_rows(rmid, rnear, rcode, 0, 288, 352)
    encode_rows(rmid, rnear, rcode, 1, 272, 336)
    found = product(rcode, ((0, 8), (32, 8)), fwd_hi, fwd_lo).reshape(8, 2, 8, 256)
    for k in range(2):
        nums[k, 0:4] = found[0:4, k]
        nums[k, 16:20] = found[4:8, k]
    for at in (0, 16):
        remote(nums.at[1 - c, at : at + 4], r_core.at[at : at + 4], "swap2", partner).start()

    def normal(line):
        cover = iota((128, 256), 1) + iota((128, 256), 0) - 15
        valid = ((cover >= 0) & (cover < 256) & (iota((128, 256), 0) < 31)).astype(F32)
        return block_swap(jnp.dot(line, valid, precision=HI, preferred_element_type=F32))

    def total_of(own_part, parts):
        total = own_part
        for i in range(15):
            total = total + parts[i]
        return total

    got(q_in, "qsum")
    norm = normal(total_of(q_sum[u + 2], q_in))
    pair = jnp.where(extra, extra_pair(u), 0)

    @pl.when(extra)
    def _():
        got(qx_in, "qx")
        norms[...] = normal(total_of(q_sum[pair], qx_in))

    got(r_core.at[0:8], "swap2")
    for at in (0, 16):
        a_sum[at : at + 4] = nums[c, at : at + 4] + r_core[at : at + 4]
    for d, copy, x_copy in zip(AWAY, spread, x_spread):
        when(at_edge(chip(d)), copy.start)
        when(is_extra(chip(d)), x_copy.start)

    got(r_in, "rs1")
    model[c, u + 2] = own[c, u] * total_of(a_sum[u + 2], r_in) / norm

    mine = model.at[c, u + 2]
    for d in AWAY:
        remote(mine, mine, "ag2", there(d), 4 + z).start()

    @pl.when(extra)
    def _():
        got(x_in, "x")
        before = prev[c, jnp.where(u < 8, u - 3, 2)]
        after = follow[c, jnp.where(u < 8, 0, u - 9)]
        exists = jnp.where(u < 8, has_down.astype(jnp.int32), has_up.astype(jnp.int32)) > 0
        old = jnp.where(u < 8, before, after)
        new = old * total_of(a_sum[pair], x_in) / norms[...]
        model[c, pair] = jnp.where(exists, new, 0.0)
        block = model.at[c, pair]
        for d in AWAY:
            remote(block, block, "xg", there(d)).start()

    for row in (1, 2, 0, 3):
        got_row(model, row, "ag2_%d" % row)
        part = model.at[c, 4 * row + 2 : 4 * row + 6]
        remote(part, part, "hand2", partner).start()
    when(extra, lambda: got(model.at[c, 0:3], "xg"))
    when(jnp.logical_not(extra), lambda: got(model.at[c, 0:4], "xg"))
    for at in (0, 18):
        part = model.at[c, at : at + 2]
        remote(part, part, "hand2", partner).start()
    got(model.at[c], "hand2")

    for g in range(5):
        put(weave(model, 4 * g, 4), 64 * g, mid, near)
    encode_rows(mid, near, code, 0, 0, 320)
    encode_rows(mid, near, code, 1, 0, 304)
    blurred = product(code, ((0, 36),), flip_hi, flip_lo)
    for low, count, weight, comes in ((0, 2, w_down, has_down), (2, 32, w_here, None), (34, 2, w_up, has_up)):
        for g in range(low, low + count, 4):
            n = min(4, low + count - g)
            value = weight * expo[g + 4 : g + 4 + n].reshape(8 * n, 256) / blurred[8 * g : 8 * g + 8 * n]
            if comes is not None:
                value = jnp.where(comes, value, 0.0)
            hmid[g // 2 : (g + n) // 2] = value.reshape(n // 2, 2, 8, 256)
            hnear[g // 2 : (g + n) // 2] = beside(value).reshape(n // 2, 2, 8, 256)
    for parity in range(2):
        for shift, count in ((0, 18), (1, 16)):
            for k, src in ((0, hmid), (1, hnear)):
                value = src[shift : shift + count, parity].reshape(8 * count, 256)
                lanes = slice(256 * k, 256 * k + 256)
                encode(value, hcode.at[parity, shift], slice(0, 8 * count), lanes)
    nums2[0] = product_half(hcode, 1 - c, fwd_hi, fwd_lo).reshape(16, 8, 256)
    remote(nums2.at[0], r_core2, "swap3", partner).start()
    nums2[1] = product_half(hcode, c, fwd_hi, fwd_lo).reshape(16, 8, 256)
    got(r_core2, "swap3")
    a_sum2[...] = nums2[1] + r_core2[...]
    for i, d in enumerate(AWAY):
        remote(a_sum2.at[chip(d)], r_in2.at[i], "rs2", there(d)).start()
    got(r_in2, "rs2")
    out_ref[...] = block_swap(model[c, u + 2] * total_of(a_sum2[u], r_in2) / norm)

    for name in ("ag1", "rs1", "ag2", "rs2"):
        gone(r_in, name)
    gone(own.at[c], "hand1")
    gone(q_core, "qswap")
    gone(q_in, "qsum")
    gone(r_core.at[4:16], "swap1")
    gone(r_core.at[0:8], "swap2")
    gone(model.at[c], "hand2")
    gone(r_core2, "swap3")
    for ref, name in ((q_in, "qx"), (x_in, "x")):
        when(extra, lambda ref=ref, name=name: gone(ref.at[0:3], name))
        when(jnp.logical_not(extra), lambda ref=ref, name=name: gone(ref.at[0:4], name))
    when(extra, lambda: gone(x_in, "xg"))
    when(has_up, lambda: gone(exp_prev, "edge0"))
    when(has_down, lambda: gone(exp_follow, "edge1"))
    when(last & has_up, lambda: gone(prev.at[c, 0], "hop0"))
    when(first & has_down, lambda: gone(prev.at[c, 0], "hop1"))
    when(last & has_down, lambda: gone(x_in, "relay0"))
    when(first & has_up, lambda: gone(x_in, "relay1"))
    when(has_down, lambda: gone(prev.at[c], "pass0"))
    when(has_up, lambda: gone(prev.at[c], "pass1"))


def body(exposures, sky_model, blur_kernels, coverage):
    vmem = pl.BlockSpec(memory_space=pltpu.VMEM)
    V = pltpu.VMEM
    D = pltpu.SemaphoreType.DMA
    op = V((7, 2, 8, 32, 256), BF)

    def blocks(*dims):
        return V((*dims, 8, 256), F32)

    def lanes(*dims):
        return V((*dims, 8, 128), F32)

    return pl.pallas_call(
        kernel,
        out_shape=jax.ShapeDtypeStruct((8, 256), F32),
        in_specs=[pl.BlockSpec(memory_space=pl.ANY)] * 4,
        out_specs=vmem,
        scratch_shapes=[
            V((256, 256), F32), V((8, 256), F32), V((31, 1, 31), F32), pltpu.SMEM((1, 8), jnp.int32),
            V((32, 128), F32), V((48, 128), F32), op, op, op, op,
            V((384, 256), F32), V((384, 256), F32), V((352, 256), F32), V((352, 256), F32),
            blocks(18, 2), blocks(18, 2), V((2, 2, 384, 512), BF), V((2, 2, 352, 512), BF), V((2, 2, 2, 144, 512), BF),
            blocks(2, 16), blocks(2, 4), blocks(2, 4), blocks(2, 20), V((48, 256), F32), V((48, 256), F32), blocks(44),
            V((8, 256), F32),
            lanes(2, 20), lanes(20), lanes(20), lanes(15), lanes(15),
            blocks(2, 20), blocks(20), blocks(20), blocks(15), blocks(15), blocks(2, 16), blocks(16), blocks(16), blocks(15),
            D((4,)), D((len(SENDS),)), D((len(ARRIVALS),)),
        ],
        compiler_params=pltpu.CompilerParams(collective_id=0, has_side_effects=True),
    )(exposures, sky_model, jnp.transpose(blur_kernels, (1, 0, 2)), coverage)


def solution(mesh):
    return jax.shard_map(
        body,
        mesh=mesh,
        in_specs=(
            P("visit", "tile", None),
            P(("tile", "visit"), None),
            P("visit", None, None),
            P("visit", None),
        ),
        out_specs=P(("tile", "visit"), None),
        check_vma=False,
    )
```

```python
import jax
import jax.numpy as jnp
from jax import lax
from jax.experimental import pallas as pl
from jax.experimental.pallas import tpu as pltpu
from jax.sharding import PartitionSpec as P

F32 = jnp.float32
BF = jnp.bfloat16
HI = lax.Precision.HIGHEST
MESH = pl.DeviceIdType.MESH
ITERS = 2


def iota(shape, dim):
    return lax.broadcasted_iota(jnp.int32, shape, dim)


def block_swap(x):
    s = iota((8, 256), 0)
    b = iota((8, 256), 1) // 32
    out = x
    for d in range(1, 8):
        moved = pltpu.roll(pltpu.roll(x, d, 0), 256 - 32 * d, 1)
        out = jnp.where((s - b) % 8 == d, moved, out)
    return out


def build_rows(k, rows):
    rows[...] = jnp.zeros_like(rows)
    m = iota((128, 128), 1)
    b = iota((128, 128), 0)
    for r in range(4):
        pick = ((m == (32 * r - 1 - b + 256) % 128) & (b < 31)).astype(F32)
        moved = jnp.dot(k, pick, precision=HI, preferred_element_type=F32)
        rows[5 + r : 37 + r, :] = rows[5 + r : 37 + r, :] + moved


def build_operator(rows, op_hi, op_lo):
    c2 = iota((64, 128), 0)
    b = c2 - 1 - iota((64, 128), 1) % 32
    inside = (b >= 0) & (b <= 30)

    def step(j, carry):
        wide = jnp.broadcast_to(rows[pl.ds(j, 1), :], (8, 128))
        base = pltpu.roll(wide, 0, 1, stride=1, stride_axis=0)
        value = jnp.concatenate([base] + [pltpu.roll(base, 8 * i, 1) for i in range(1, 8)], axis=0)
        value = jnp.where(inside, value, 0.0)
        hi = value.astype(BF)
        lo = (value - hi.astype(F32)).astype(BF)
        for shift, lanes in ((4, slice(0, 128)), (8, slice(128, 256))):
            o, r = (j + shift) // 8, (j + shift) % 8
            for op, x in ((op_hi, hi), (op_lo, lo)):
                op[o, 0, r, :, lanes] = x[16:48]
                op[o, 1, r, 0:16, lanes] = x[48:64]
                op[o, 1, r, 16:32, lanes] = x[0:16]
        return carry

    lax.fori_loop(0, 44, step, 0, unroll=11)


def beside(value):
    n = value.shape[0]
    group = iota(value.shape, 0) % 8
    before = jnp.where(group > 0, pltpu.roll(value, 1, 0), 0.0)
    after = jnp.where(group < 7, pltpu.roll(value, n - 1, 0), 0.0)
    return jnp.where(iota(value.shape, 1) % 32 < 16, after, before)


def put(value, first, mid, near):
    n = value.shape[0]
    mid[first : first + n, :] = value
    near[first : first + n, :] = beside(value)


def weave(ref, first, count):
    pairs = [ref[0, first : first + count], ref[1, first : first + count]]
    return jnp.stack(pairs, axis=1).reshape(16 * count, 256)


def encode(value, code, rows, lanes):
    hi = value.astype(BF)
    code[0, rows, lanes] = hi
    code[1, rows, lanes] = (value - hi.astype(F32)).astype(BF)


def encode_rows(mid, near, code, shift, first, last):
    for at in range(first, last, 64):
        n = min(64, last - at)
        for k, src in ((0, mid), (1, near)):
            rows = slice(at + 8 * shift, at + 8 * shift + n)
            encode(src[rows, :], code.at[shift], slice(at, at + n), slice(256 * k, 256 * k + 256))


def multiply(left, op_hi, op_lo):
    def dot(x, op):
        return jnp.dot(x, op[1:6].reshape(2560, 256), preferred_element_type=F32)

    hi, lo = left
    return dot(hi, op_hi) + (dot(hi, op_lo) + dot(lo, op_hi))


def product(code, ranges, op_hi, op_lo):
    left = []
    for term in range(2):
        parts = []
        for first, count in ranges:
            at = [8 * first + 16 * (o // 2) for o in range(5)]
            parts.append(
                jnp.concatenate([code[o % 2, term, at[o] : at[o] + 8 * count, :] for o in range(5)], axis=1)
            )
        left.append(jnp.concatenate(parts, axis=0) if len(parts) > 1 else parts[0])
    return multiply(left, op_hi, op_lo)


def far(d):
    return -(d[0] + (2 if d[1] == 2 else 1 if d[1] else 0))


AWAY = sorted([(dz, dy) for dz in range(4) for dy in range(4) if (dz, dy) != (0, 0)], key=far)
SENDS = ("ag1", "hand1", "qswap", "qsum", "qx", "swap1", "swap2", "rs1", "x", "ag2", "hand2", "xg", "swap3", "rs2")
SENDS += ("ag2o", "xgo", "swap4", "hop0", "hop1", "relay0", "relay1", "pass0", "pass1", "edge0", "edge1")
ARRIVALS = ("ag1_0", "ag1_1", "ag1_2", "ag1_3", "ag2_0", "ag2_1", "ag2_2", "ag2_3", "ag2_late") + SENDS


def is_extra(u):
    return (u == 5) | (u == 6) | (u == 9) | (u == 10)


def extra_pair(u):
    return jnp.where(u < 8, u - 5, u + 9)


def kernel(
    exp_hbm, sky_hbm, ker_hbm, cov_hbm, out_ref,
    exp_ref, sky_ref, ker_ref, cov_ref, kpad, rows, fwd_hi, fwd_lo, flip_hi, flip_lo, mid, near, rmid, rnear, code, rcode,
    own, prev, follow, model, exp_prev, exp_follow, expo, norms,
    q_all, q_core, q_sum, q_in, qx_in, nums, r_core, a_sum, r_in, x_in, nums2, r_core2, a_sum2, r_in2,
    load_sems, send_sems, recv_sems,
):
    t = lax.axis_index("tile")
    v = lax.axis_index("visit")
    tiles = lax.axis_size("tile")
    z, y, c = v // 8, (v // 2) % 4, v % 2
    u = v // 2

    def chip(d):
        return ((z + d[0]) % 4) * 4 + (y + d[1]) % 4

    def there(d):
        return {"visit": 2 * chip(d) + c, "tile": t}

    def across(d):
        return {"visit": 2 * chip(d) + 1 - c, "tile": t}

    partner = {"visit": 2 * u + (1 - c), "tile": t}
    up = {"visit": v, "tile": t + 1}
    down = {"visit": v, "tile": t - 1}
    has_up = t < tiles - 1
    has_down = t > 0
    extra = is_extra(u)

    def at_edge(place):
        return (place < 2) | (place >= 14)

    late = at_edge(u)

    loads = [
        pltpu.make_async_copy(src, dst, load_sems.at[i])
        for i, (src, dst) in enumerate(
            ((ker_hbm, ker_ref), (cov_hbm, cov_ref), (sky_hbm, sky_ref), (exp_hbm.at[0], exp_ref))
        )
    ]
    for copy in loads:
        copy.start()
    prev[...] = jnp.zeros_like(prev)
    follow[...] = jnp.zeros_like(follow)
    barrier = pltpu.get_barrier_semaphore()
    for peer in [there(d) for d in AWAY] + [partner]:
        pl.semaphore_signal(barrier, inc=1, device_id=peer, device_id_type=MESH)

    @pl.when(has_up)
    def _():
        pl.semaphore_signal(barrier, inc=1, device_id=up, device_id_type=MESH)

    @pl.when(has_down)
    def _():
        pl.semaphore_signal(barrier, inc=1, device_id=down, device_id_type=MESH)

    def remote(src, dst, name, device, arrival=None):
        return pltpu.make_async_remote_copy(
            src_ref=src,
            dst_ref=dst,
            send_sem=send_sems.at[SENDS.index(name)],
            recv_sem=recv_sems.at[ARRIVALS.index(name) if arrival is None else arrival],
            device_id=device,
            device_id_type=MESH,
        )

    def got(ref, name):
        remote(ref, ref, "ag1", partner, ARRIVALS.index(name)).wait_recv()

    def gone(ref, name):
        remote(ref, ref, name, partner).wait_send()

    def when(cond, act):
        pl.when(cond)(act)

    kpad[...] = jnp.zeros_like(kpad)
    loads[0].wait()
    raw = ker_ref[:, 0, :]
    kpad[0:31, 0:31] = raw / jnp.sum(raw)
    loads[1].wait()
    w_here = cov_ref[0, t].astype(F32)
    w_down = jnp.where(has_down, cov_ref[0, jnp.maximum(t - 1, 0)], 0).astype(F32)
    w_up = jnp.where(has_up, cov_ref[0, jnp.minimum(t + 1, tiles - 1)], 0).astype(F32)
    i128, a32 = iota((128, 32), 0), iota((128, 32), 1)
    weights = jnp.where(
        i128 < 64,
        jnp.where(i128 + a32 < 47, w_down, w_here),
        jnp.where(i128 + a32 >= 111, w_up, w_here),
    )
    lines = jnp.dot(weights, kpad[...], precision=HI, preferred_element_type=F32)
    for b in range(40):
        at = 8 * b if b < 8 else 64 + 8 * (b - 32) if b >= 32 else 48
        q_all[b % 2, b // 2] = lines[at : at + 8]
    loads[2].wait()
    own[c, u] = block_swap(sky_ref[...])
    turn_rows = (iota((32, 32), 0) + iota((32, 32), 1) == 30).astype(F32)
    turn_cols = (iota((128, 128), 0) + iota((128, 128), 1) == 30).astype(F32)
    turned = jnp.dot(turn_rows, kpad[...], precision=HI, preferred_element_type=F32)
    turned = jnp.dot(turned, turn_cols, precision=HI, preferred_element_type=F32)
    build_rows(turned, rows)
    build_operator(rows, flip_hi, flip_lo)

    pl.semaphore_wait(barrier, 16 + has_up.astype(jnp.int32) + has_down.astype(jnp.int32))

    edge_up = remote(exp_ref.at[208:256, :], exp_prev, "edge0", up)
    edge_down = remote(exp_ref.at[0:48, :], exp_follow, "edge1", down)
    mine = own.at[c, u]
    hop_up = remote(mine, prev.at[c, u % 4], "hop0", up)
    hop_down = remote(mine, follow.at[c, u % 4], "hop1", down)
    last = u >= 12
    first = u < 4

    def relay_up():
        got(prev.at[c, u % 4], "hop0")
        block = prev.at[c, u % 4]
        for d in AWAY:
            remote(block, block, "relay0", there(d)).start()

    def relay_down():
        got(follow.at[c, u % 4], "hop1")
        block = follow.at[c, u % 4]
        for d in AWAY:
            remote(block, block, "relay1", there(d)).start()

    def hand_over(halo, name, relayed, comes, relayer):
        when(comes & relayer, lambda: got(halo.at[c, 0:3], relayed))
        when(comes & jnp.logical_not(relayer), lambda: got(halo.at[c], relayed))
        when(comes, lambda: remote(halo.at[c], halo.at[c], name, partner).start())

    when(last & has_up, hop_up.start)
    when(first & has_down, hop_down.start)
    for d in AWAY:
        remote(mine, mine, "ag1", there(d), z).start()
    remote(q_all.at[1 - c], q_core, "qswap", partner).start()
    loads[3].wait()
    when(has_up, edge_up.start)
    when(has_down, edge_down.start)
    build_rows(kpad[...], rows)
    build_operator(rows, fwd_hi, fwd_lo)
    when(last & has_down, relay_up)
    when(first & has_up, relay_down)

    def swap_exposure(i, carry):
        for j in range(4):
            at = pl.multiple_of(32 * i + 8 * j, 8)
            expo[4 * i + j + 6] = block_swap(exp_ref[pl.ds(at, 8), :])
        return carry

    lax.fori_loop(0, 8, swap_exposure, 0)

    def got_row(ref, row, name):
        when(z == row, lambda: got(ref.at[c, 0:3], name))
        when(z != row, lambda: got(ref.at[c, 0:4], name))

    for row in (1, 2, 0, 3):
        got_row(own, row, "ag1_%d" % row)
        part = own.at[c, 4 * row : 4 * row + 4]
        remote(part, part, "hand1", partner).start()
    got(own.at[c], "hand1")

    for g in range(4):
        put(weave(own, 4 * g, 4), 64 + 64 * g, mid, near)
    encode_rows(mid, near, code, 0, 64, 320)
    encode_rows(mid, near, code, 1, 64, 304)
    blurred = product(code, ((8, 28),), flip_hi, flip_lo)
    value = w_here * expo[8:36].reshape(224, 256) / blurred
    for g in range(7):
        put(value[32 * g : 32 * g + 32], 64 + 32 * g, rmid, rnear)
    encode_rows(rmid, rnear, rcode, 0, 64, 288)
    encode_rows(rmid, rnear, rcode, 1, 64, 272)

    got(q_core, "qswap")
    q_sum[...] = q_all[c] + q_core[...]
    for i, d in enumerate(AWAY):
        remote(q_sum.at[chip(d) + 2], q_in.at[i], "qsum", there(d)).start()
    for i, d in enumerate(AWAY):
        when(is_extra(chip(d)), remote(q_sum.at[extra_pair(chip(d))], qx_in.at[i], "qx", there(d)).start)

    far_prev = t == tiles // 2
    far_follow = t == tiles // 2 - 1
    hand_over(prev, "pass0", "relay0", has_down & jnp.logical_not(far_prev), last)
    hand_over(follow, "pass1", "relay1", has_up & jnp.logical_not(far_follow), first)
    found = product(rcode, ((8, 24),), fwd_hi, fwd_lo).reshape(12, 2, 8, 256)
    for k in range(2):
        nums[k, 4:16] = found[:, k]
    remote(nums.at[1 - c, 4:16], r_core.at[4:16], "swap1", partner).start()
    hand_over(prev, "pass0", "relay0", far_prev, last)
    hand_over(follow, "pass1", "relay1", far_follow, first)

    when(has_down, lambda: got(exp_prev, "edge0"))
    when(has_up, lambda: got(exp_follow, "edge1"))

    def swap_edges(i, carry):
        at = pl.multiple_of(8 * i, 8)
        expo[i] = block_swap(exp_prev[pl.ds(at, 8), :])
        expo[38 + i] = block_swap(exp_follow[pl.ds(at, 8), :])
        return carry

    lax.fori_loop(0, 6, swap_edges, 0, unroll=2)
    got(r_core.at[4:16], "swap1")
    a_sum[4:16] = nums[c, 4:16] + r_core[4:16]

    spread = [remote(a_sum.at[chip(d) + 2], r_in.at[i], "rs1", there(d)) for i, d in enumerate(AWAY)]
    x_spread = [remote(a_sum.at[extra_pair(chip(d))], x_in.at[i], "x", there(d)) for i, d in enumerate(AWAY)]
    for d, copy in zip(AWAY, spread):
        when(jnp.logical_not(at_edge(chip(d))), copy.start)

    when(has_down, lambda: got(prev.at[1 - c], "pass0"))
    when(has_up, lambda: got(follow.at[1 - c], "pass1"))
    put(weave(prev, 0, 4), 0, mid, near)
    put(weave(follow, 0, 4), 320, mid, near)
    encode_rows(mid, near, code, 0, 0, 64)
    encode_rows(mid, near, code, 1, 0, 64)
    encode_rows(mid, near, code, 0, 320, 384)
    encode_rows(mid, near, code, 1, 304, 368)
    blurred = product(code, ((0, 8), (36, 8)), flip_hi, flip_lo)
    for low, source, count, weight, comes in (
        (0, 0, 6, w_down, has_down),
        (6, 48, 2, w_here, None),
        (36, 64, 2, w_here, None),
        (38, 80, 6, w_up, has_up),
    ):
        m = 8 * count
        value = weight * expo[low : low + count].reshape(m, 256) / blurred[source : source + m]
        if comes is not None:
            value = jnp.where(comes, value, 0.0)
        put(value, 8 * low, rmid, rnear)
    encode_rows(rmid, rnear, rcode, 0, 0, 64)
    encode_rows(rmid, rnear, rcode, 1, 0, 64)
    encode_rows(rmid, rnear, rcode, 0, 288, 352)
    encode_rows(rmid, rnear, rcode, 1, 272, 336)
    found = product(rcode, ((0, 8), (32, 8)), fwd_hi, fwd_lo).reshape(8, 2, 8, 256)
    for k in range(2):
        nums[k, 0:4] = found[0:4, k]
        nums[k, 16:20] = found[4:8, k]
    for at in (0, 16):
        remote(nums.at[1 - c, at : at + 4], r_core.at[at : at + 4], "swap2", partner).start()

    def normal(line):
        cover = iota((128, 256), 1) + iota((128, 256), 0) - 15
        valid = ((cover >= 0) & (cover < 256) & (iota((128, 256), 0) < 31)).astype(F32)
        return block_swap(jnp.dot(line, valid, precision=HI, preferred_element_type=F32))

    def total_of(own_part, parts):
        total = own_part
        for i in range(15):
            total = total + parts[i]
        return total

    got(q_in, "qsum")
    norm = normal(total_of(q_sum[u + 2], q_in))
    pair = jnp.where(extra, extra_pair(u), 0)

    @pl.when(extra)
    def _():
        got(qx_in, "qx")
        norms[...] = normal(total_of(q_sum[pair], qx_in))

    got(r_core.at[0:8], "swap2")
    for at in (0, 16):
        a_sum[at : at + 4] = nums[c, at : at + 4] + r_core[at : at + 4]
    for d, copy, x_copy in zip(AWAY, spread, x_spread):
        when(at_edge(chip(d)), copy.start)
        when(is_extra(chip(d)), x_copy.start)

    got(r_in, "rs1")
    model[c, u + 2] = own[c, u] * total_of(a_sum[u + 2], r_in) / norm

    mine = model.at[c, u + 2]
    arrival = jnp.where(late, ARRIVALS.index("ag2_late"), ARRIVALS.index("ag2_0") + z)
    for d in AWAY:
        remote(mine, mine, "ag2", there(d), arrival).start()

    @pl.when(late)
    def _():
        for d in AWAY + [(0, 0)]:
            remote(mine, mine, "ag2o", across(d)).start()

    @pl.when(extra)
    def _():
        got(x_in, "x")
        before = prev[c, jnp.where(u < 8, u - 3, 2)]
        after = follow[c, jnp.where(u < 8, 0, u - 9)]
        exists = jnp.where(u < 8, has_down.astype(jnp.int32), has_up.astype(jnp.int32)) > 0
        old = jnp.where(u < 8, before, after)
        new = old * total_of(a_sum[pair], x_in) / norms[...]
        model[c, pair] = jnp.where(exists, new, 0.0)
        block = model.at[c, pair]
        for d in AWAY:
            remote(block, block, "xg", there(d)).start()
        for d in AWAY + [(0, 0)]:
            remote(block, block, "xgo", across(d)).start()

    def got_all(ref, count, mine_too, name):
        when(mine_too, lambda: got(ref.at[c, 0 : count - 1], name))
        when(jnp.logical_not(mine_too), lambda: got(ref.at[c, 0:count], name))

    for row, low, high in ((1, 6, 10), (2, 10, 14), (0, 4, 6), (3, 14, 16)):
        got_all(model, high - low, (z == row) & jnp.logical_not(late), "ag2_%d" % row)
        part = model.at[c, low:high]
        remote(part, part, "hand2", partner).start()
    got(model.at[c, 0:12], "hand2")
    for g in range(3):
        put(weave(model, 4 + 4 * g, 4), 64 + 64 * g, mid, near)
    encode_rows(mid, near, code, 0, 64, 256)
    encode_rows(mid, near, code, 1, 64, 240)
    blurred = product(code, ((8, 20),), flip_hi, flip_lo)
    value = w_here * expo[12:32].reshape(160, 256) / blurred
    for g in range(5):
        put(value[32 * g : 32 * g + 32], 64 + 32 * g, rmid, rnear)
    encode_rows(rmid, rnear, rcode, 0, 64, 224)
    encode_rows(rmid, rnear, rcode, 1, 64, 208)
    found = product(rcode, ((8, 16),), fwd_hi, fwd_lo).reshape(8, 2, 8, 256)
    for k in range(2):
        nums2[k, 4:12] = found[:, k]
    remote(nums2.at[1 - c, 4:12], r_core2.at[4:12], "swap3", partner).start()
    got(r_core2.at[4:12], "swap3")
    a_sum2[4:12] = nums2[c, 4:12] + r_core2[4:12]
    spread = [remote(a_sum2.at[chip(d)], r_in2.at[i], "rs2", there(d)) for i, d in enumerate(AWAY)]

    def inner(place):
        return (place >= 4) & (place < 12)

    for d, copy in zip(AWAY, spread):
        when(inner(chip(d)), copy.start)

    got_all(model, 4, late, "ag2_late")
    got_all(model, 4, extra, "xg")
    got(model.at[c, 0:4], "ag2o")
    got(model.at[c, 0:4], "xgo")
    put(weave(model, 0, 4), 0, mid, near)
    put(weave(model, 16, 4), 256, mid, near)
    encode_rows(mid, near, code, 0, 0, 64)
    encode_rows(mid, near, code, 1, 0, 64)
    encode_rows(mid, near, code, 0, 256, 320)
    encode_rows(mid, near, code, 1, 240, 304)
    blurred = product(code, ((0, 8), (28, 8)), flip_hi, flip_lo)
    for low, source, count, weight, comes in (
        (0, 0, 2, w_down, has_down),
        (2, 16, 6, w_here, None),
        (28, 64, 6, w_here, None),
        (34, 112, 2, w_up, has_up),
    ):
        m = 8 * count
        value = weight * expo[low + 4 : low + 4 + count].reshape(m, 256) / blurred[source : source + m]
        if comes is not None:
            value = jnp.where(comes, value, 0.0)
        put(value, 8 * low, rmid, rnear)
    encode_rows(rmid, rnear, rcode, 0, 0, 64)
    encode_rows(rmid, rnear, rcode, 1, 0, 64)
    encode_rows(rmid, rnear, rcode, 0, 224, 288)
    encode_rows(rmid, rnear, rcode, 1, 208, 272)
    found = product(rcode, ((0, 8), (24, 8)), fwd_hi, fwd_lo).reshape(8, 2, 8, 256)
    for k in range(2):
        nums2[k, 0:4] = found[0:4, k]
        nums2[k, 12:16] = found[4:8, k]
    for at in (0, 12):
        remote(nums2.at[1 - c, at : at + 4], r_core2.at[at : at + 4], "swap4", partner).start()
    got(r_core2.at[0:8], "swap4")
    for at in (0, 12):
        a_sum2[at : at + 4] = nums2[c, at : at + 4] + r_core2[at : at + 4]
    for d, copy in zip(AWAY, spread):
        when(jnp.logical_not(inner(chip(d))), copy.start)
    got(r_in2, "rs2")
    out_ref[...] = block_swap(model[c, u + 2] * total_of(a_sum2[u], r_in2) / norm)

    for name in ("ag1", "rs1", "ag2", "rs2"):
        gone(r_in, name)
    gone(own.at[c], "hand1")
    gone(q_core, "qswap")
    gone(q_in, "qsum")
    gone(r_core.at[4:16], "swap1")
    gone(r_core.at[0:8], "swap2")
    gone(model.at[c, 0:12], "hand2")
    gone(r_core2.at[0:8], "swap3")
    gone(r_core2.at[0:8], "swap4")
    when(late, lambda: gone(r_core2, "ag2o"))
    when(extra, lambda: gone(r_core2, "xgo"))
    for ref, name in ((q_in, "qx"), (x_in, "x")):
        when(extra, lambda ref=ref, name=name: gone(ref.at[0:3], name))
        when(jnp.logical_not(extra), lambda ref=ref, name=name: gone(ref.at[0:4], name))
    when(extra, lambda: gone(x_in, "xg"))
    when(has_up, lambda: gone(exp_prev, "edge0"))
    when(has_down, lambda: gone(exp_follow, "edge1"))
    when(last & has_up, lambda: gone(prev.at[c, 0], "hop0"))
    when(first & has_down, lambda: gone(prev.at[c, 0], "hop1"))
    when(last & has_down, lambda: gone(x_in, "relay0"))
    when(first & has_up, lambda: gone(x_in, "relay1"))
    when(has_down, lambda: gone(prev.at[c], "pass0"))
    when(has_up, lambda: gone(prev.at[c], "pass1"))


def body(exposures, sky_model, blur_kernels, coverage):
    vmem = pl.BlockSpec(memory_space=pltpu.VMEM)
    V = pltpu.VMEM
    D = pltpu.SemaphoreType.DMA
    op = V((7, 2, 8, 32, 256), BF)

    def blocks(*dims):
        return V((*dims, 8, 256), F32)

    def lanes(*dims):
        return V((*dims, 8, 128), F32)

    return pl.pallas_call(
        kernel,
        out_shape=jax.ShapeDtypeStruct((8, 256), F32),
        in_specs=[pl.BlockSpec(memory_space=pl.ANY)] * 4,
        out_specs=vmem,
        scratch_shapes=[
            V((256, 256), F32), V((8, 256), F32), V((31, 1, 31), F32), pltpu.SMEM((1, 8), jnp.int32),
            V((32, 128), F32), V((48, 128), F32), op, op, op, op,
            V((384, 256), F32), V((384, 256), F32), V((352, 256), F32), V((352, 256), F32),
            V((2, 2, 384, 512), BF), V((2, 2, 352, 512), BF),
            blocks(2, 16), blocks(2, 4), blocks(2, 4), blocks(2, 20), V((48, 256), F32), V((48, 256), F32), blocks(44),
            V((8, 256), F32),
            lanes(2, 20), lanes(20), lanes(20), lanes(15), lanes(15),
            blocks(2, 20), blocks(20), blocks(20), blocks(15), blocks(15), blocks(2, 16), blocks(16), blocks(16), blocks(15),
            D((4,)), D((len(SENDS),)), D((len(ARRIVALS),)),
        ],
        compiler_params=pltpu.CompilerParams(collective_id=0, has_side_effects=True),
    )(exposures, sky_model, jnp.transpose(blur_kernels, (1, 0, 2)), coverage)


def solution(mesh):
    return jax.shard_map(
        body,
        mesh=mesh,
        in_specs=(
            P("visit", "tile", None),
            P(("tile", "visit"), None),
            P("visit", None, None),
            P("visit", None),
        ),
        out_specs=P(("tile", "visit"), None),
        check_vma=False,
    )
```

```python
import jax
import jax.numpy as jnp
from jax import lax
from jax.experimental import pallas as pl
from jax.experimental.pallas import tpu as pltpu
from jax.sharding import PartitionSpec as P

F32 = jnp.float32
BF = jnp.bfloat16
HI = lax.Precision.HIGHEST
MESH = pl.DeviceIdType.MESH
ITERS = 2


def iota(shape, dim):
    return lax.broadcasted_iota(jnp.int32, shape, dim)


def block_swap(x):
    s = iota((8, 256), 0)
    b = iota((8, 256), 1) // 32
    out = x
    for d in range(1, 8):
        moved = pltpu.roll(pltpu.roll(x, d, 0), 256 - 32 * d, 1)
        out = jnp.where((s - b) % 8 == d, moved, out)
    return out


def build_rows(k, rows):
    rows[...] = jnp.zeros_like(rows)
    m = iota((128, 128), 1)
    b = iota((128, 128), 0)
    for r in range(4):
        pick = ((m == (32 * r - 1 - b + 256) % 128) & (b < 31)).astype(F32)
        moved = jnp.dot(k, pick, precision=HI, preferred_element_type=F32)
        rows[5 + r : 37 + r, :] = rows[5 + r : 37 + r, :] + moved


def build_operator(rows, op_hi, op_lo):
    c2 = iota((64, 128), 0)
    b = c2 - 1 - iota((64, 128), 1) % 32
    inside = (b >= 0) & (b <= 30)

    def step(j, carry):
        wide = jnp.broadcast_to(rows[pl.ds(j, 1), :], (8, 128))
        base = pltpu.roll(wide, 0, 1, stride=1, stride_axis=0)
        value = jnp.concatenate([base] + [pltpu.roll(base, 8 * i, 1) for i in range(1, 8)], axis=0)
        value = jnp.where(inside, value, 0.0)
        hi = value.astype(BF)
        lo = (value - hi.astype(F32)).astype(BF)
        for shift, lanes in ((4, slice(0, 128)), (8, slice(128, 256))):
            o, r = (j + shift) // 8, (j + shift) % 8
            for op, x in ((op_hi, hi), (op_lo, lo)):
                op[o, 0, r, :, lanes] = x[16:48]
                op[o, 1, r, 0:16, lanes] = x[48:64]
                op[o, 1, r, 16:32, lanes] = x[0:16]
        return carry

    lax.fori_loop(0, 44, step, 0, unroll=11)


def beside(value):
    n = value.shape[0]
    group = iota(value.shape, 0) % 8
    before = jnp.where(group > 0, pltpu.roll(value, 1, 0), 0.0)
    after = jnp.where(group < 7, pltpu.roll(value, n - 1, 0), 0.0)
    return jnp.where(iota(value.shape, 1) % 32 < 16, after, before)


def put(value, first, mid, near):
    n = value.shape[0]
    mid[first : first + n, :] = value
    near[first : first + n, :] = beside(value)


def weave(ref, first, count):
    pairs = [ref[0, first : first + count], ref[1, first : first + count]]
    return jnp.stack(pairs, axis=1).reshape(16 * count, 256)


def encode(value, code, rows, lanes):
    hi = value.astype(BF)
    code[0, rows, lanes] = hi
    code[1, rows, lanes] = (value - hi.astype(F32)).astype(BF)


def encode_rows(mid, near, code, shift, first, last):
    for at in range(first, last, 64):
        n = min(64, last - at)
        for k, src in ((0, mid), (1, near)):
            rows = slice(at + 8 * shift, at + 8 * shift + n)
            encode(src[rows, :], code.at[shift], slice(at, at + n), slice(256 * k, 256 * k + 256))


def multiply(left, op_hi, op_lo):
    def dot(x, op):
        return jnp.dot(x, op[1:6].reshape(2560, 256), preferred_element_type=F32)

    hi, lo = left
    return dot(hi, op_hi) + (dot(hi, op_lo) + dot(lo, op_hi))


def product(code, ranges, op_hi, op_lo):
    left = []
    for term in range(2):
        parts = []
        for first, count in ranges:
            at = [8 * first + 16 * (o // 2) for o in range(5)]
            parts.append(
                jnp.concatenate([code[o % 2, term, at[o] : at[o] + 8 * count, :] for o in range(5)], axis=1)
            )
        left.append(jnp.concatenate(parts, axis=0) if len(parts) > 1 else parts[0])
    return multiply(left, op_hi, op_lo)


def far(d):
    return -(d[0] + (2 if d[1] == 2 else 1 if d[1] else 0))


AWAY = sorted([(dz, dy) for dz in range(4) for dy in range(4) if (dz, dy) != (0, 0)], key=far)
SENDS = ("ag1", "hand1", "qswap", "qsum", "qx", "swap1", "swap2", "rs1", "x", "ag2", "hand2", "xg", "swap3", "rs2")
SENDS += ("ag2o", "xgo", "swap4", "hop0", "hop1", "relay0", "relay1", "pass0", "pass1", "edge0", "edge1")
ARRIVALS = ("ag1_0", "ag1_1", "ag1_2", "ag1_3", "ag2_0", "ag2_1", "ag2_2", "ag2_3", "ag2_late") + SENDS


def is_extra(u):
    return (u >= 6) & (u < 10)


def extra_pair(u):
    return jnp.where(u < 8, u - 6, u + 10)


def kernel(
    exp_hbm, sky_hbm, ker_hbm, cov_hbm, out_ref,
    exp_ref, sky_ref, ker_ref, cov_ref, kpad, rows, fwd_hi, fwd_lo, flip_hi, flip_lo, mid, near, rmid, rnear, code, rcode,
    own, prev, follow, model, exp_prev, exp_follow, expo, norms,
    q_all, q_core, q_sum, q_in, qx_in, nums, r_core, a_sum, r_in, x_in, nums2, r_core2, a_sum2, r_in2,
    load_sems, send_sems, recv_sems,
):
    t = lax.axis_index("tile")
    v = lax.axis_index("visit")
    tiles = lax.axis_size("tile")
    z, y, c = v // 8, (v // 2) % 4, v % 2
    u = v // 2

    def chip(d):
        return ((z + d[0]) % 4) * 4 + (y + d[1]) % 4

    def there(d):
        return {"visit": 2 * chip(d) + c, "tile": t}

    def across(d):
        return {"visit": 2 * chip(d) + 1 - c, "tile": t}

    partner = {"visit": 2 * u + (1 - c), "tile": t}
    up = {"visit": v, "tile": t + 1}
    down = {"visit": v, "tile": t - 1}
    has_up = t < tiles - 1
    has_down = t > 0
    extra = is_extra(u)

    def at_edge(place):
        return (place < 2) | (place >= 14)

    late = at_edge(u)

    loads = [
        pltpu.make_async_copy(src, dst, load_sems.at[i])
        for i, (src, dst) in enumerate(
            ((ker_hbm, ker_ref), (cov_hbm, cov_ref), (sky_hbm, sky_ref), (exp_hbm.at[0], exp_ref))
        )
    ]
    for copy in loads:
        copy.start()
    prev[...] = jnp.zeros_like(prev)
    follow[...] = jnp.zeros_like(follow)
    barrier = pltpu.get_barrier_semaphore()
    for peer in [there(d) for d in AWAY] + [partner]:
        pl.semaphore_signal(barrier, inc=1, device_id=peer, device_id_type=MESH)

    @pl.when(has_up)
    def _():
        pl.semaphore_signal(barrier, inc=1, device_id=up, device_id_type=MESH)

    @pl.when(has_down)
    def _():
        pl.semaphore_signal(barrier, inc=1, device_id=down, device_id_type=MESH)

    def remote(src, dst, name, device, arrival=None):
        return pltpu.make_async_remote_copy(
            src_ref=src,
            dst_ref=dst,
            send_sem=send_sems.at[SENDS.index(name)],
            recv_sem=recv_sems.at[ARRIVALS.index(name) if arrival is None else arrival],
            device_id=device,
            device_id_type=MESH,
        )

    def got(ref, name):
        remote(ref, ref, "ag1", partner, ARRIVALS.index(name)).wait_recv()

    def gone(ref, name):
        remote(ref, ref, name, partner).wait_send()

    def when(cond, act):
        pl.when(cond)(act)

    kpad[...] = jnp.zeros_like(kpad)
    loads[0].wait()
    raw = ker_ref[:, 0, :]
    kpad[0:31, 0:31] = raw / jnp.sum(raw)
    loads[1].wait()
    w_here = cov_ref[0, t].astype(F32)
    w_down = jnp.where(has_down, cov_ref[0, jnp.maximum(t - 1, 0)], 0).astype(F32)
    w_up = jnp.where(has_up, cov_ref[0, jnp.minimum(t + 1, tiles - 1)], 0).astype(F32)
    i128, a32 = iota((128, 32), 0), iota((128, 32), 1)
    weights = jnp.where(
        i128 < 64,
        jnp.where(i128 + a32 < 47, w_down, w_here),
        jnp.where(i128 + a32 >= 111, w_up, w_here),
    )
    lines = jnp.dot(weights, kpad[...], precision=HI, preferred_element_type=F32)
    for b in range(40):
        at = 8 * b if b < 8 else 64 + 8 * (b - 32) if b >= 32 else 48
        q_all[b % 2, b // 2] = lines[at : at + 8]
    loads[2].wait()
    own[c, u] = block_swap(sky_ref[...])
    turn_rows = (iota((32, 32), 0) + iota((32, 32), 1) == 30).astype(F32)
    turn_cols = (iota((128, 128), 0) + iota((128, 128), 1) == 30).astype(F32)
    turned = jnp.dot(turn_rows, kpad[...], precision=HI, preferred_element_type=F32)
    turned = jnp.dot(turned, turn_cols, precision=HI, preferred_element_type=F32)
    build_rows(turned, rows)
    build_operator(rows, flip_hi, flip_lo)

    pl.semaphore_wait(barrier, 16 + has_up.astype(jnp.int32) + has_down.astype(jnp.int32))

    edge_up = remote(exp_ref.at[208:256, :], exp_prev, "edge0", up)
    edge_down = remote(exp_ref.at[0:48, :], exp_follow, "edge1", down)
    mine = own.at[c, u]
    hop_up = remote(mine, prev.at[c, u % 4], "hop0", up)
    hop_down = remote(mine, follow.at[c, u % 4], "hop1", down)
    last = u >= 12
    first = u < 4

    def relay_up():
        got(prev.at[c, u % 4], "hop0")
        block = prev.at[c, u % 4]
        for d in AWAY:
            remote(block, block, "relay0", there(d)).start()

    def relay_down():
        got(follow.at[c, u % 4], "hop1")
        block = follow.at[c, u % 4]
        for d in AWAY:
            remote(block, block, "relay1", there(d)).start()

    def hand_over(halo, name, relayed, comes, relayer):
        when(comes & relayer, lambda: got(halo.at[c, 0:3], relayed))
        when(comes & jnp.logical_not(relayer), lambda: got(halo.at[c], relayed))
        when(comes, lambda: remote(halo.at[c], halo.at[c], name, partner).start())

    when(last & has_up, hop_up.start)
    when(first & has_down, hop_down.start)
    for d in AWAY:
        remote(mine, mine, "ag1", there(d), z).start()
    remote(q_all.at[1 - c], q_core, "qswap", partner).start()
    loads[3].wait()
    when(has_up, edge_up.start)
    when(has_down, edge_down.start)
    build_rows(kpad[...], rows)
    build_operator(rows, fwd_hi, fwd_lo)
    when(last & has_down, relay_up)
    when(first & has_up, relay_down)

    def swap_exposure(i, carry):
        for j in range(4):
            at = pl.multiple_of(32 * i + 8 * j, 8)
            expo[4 * i + j + 6] = block_swap(exp_ref[pl.ds(at, 8), :])
        return carry

    lax.fori_loop(0, 8, swap_exposure, 0)

    def got_row(ref, row, name):
        when(z == row, lambda: got(ref.at[c, 0:3], name))
        when(z != row, lambda: got(ref.at[c, 0:4], name))

    for row in (1, 2, 0, 3):
        got_row(own, row, "ag1_%d" % row)
        part = own.at[c, 4 * row : 4 * row + 4]
        remote(part, part, "hand1", partner).start()
    got(own.at[c], "hand1")

    for g in range(4):
        put(weave(own, 4 * g, 4), 64 + 64 * g, mid, near)
    encode_rows(mid, near, code, 0, 64, 320)
    encode_rows(mid, near, code, 1, 64, 304)
    blurred = product(code, ((8, 28),), flip_hi, flip_lo)
    value = w_here * expo[8:36].reshape(224, 256) / blurred
    for g in range(7):
        put(value[32 * g : 32 * g + 32], 64 + 32 * g, rmid, rnear)
    encode_rows(rmid, rnear, rcode, 0, 64, 288)
    encode_rows(rmid, rnear, rcode, 1, 64, 272)

    got(q_core, "qswap")
    q_sum[...] = q_all[c] + q_core[...]
    for i, d in enumerate(AWAY):
        remote(q_sum.at[chip(d) + 2], q_in.at[i], "qsum", there(d)).start()
    for i, d in enumerate(AWAY):
        when(is_extra(chip(d)), remote(q_sum.at[extra_pair(chip(d))], qx_in.at[i], "qx", there(d)).start)

    far_prev = t == tiles // 2
    far_follow = t == tiles // 2 - 1
    hand_over(prev, "pass0", "relay0", has_down & jnp.logical_not(far_prev), last)
    hand_over(follow, "pass1", "relay1", has_up & jnp.logical_not(far_follow), first)
    found = product(rcode, ((8, 24),), fwd_hi, fwd_lo).reshape(12, 2, 8, 256)
    for k in range(2):
        nums[k, 4:16] = found[:, k]
    remote(nums.at[1 - c, 4:16], r_core.at[4:16], "swap1", partner).start()
    hand_over(prev, "pass0", "relay0", far_prev, last)
    hand_over(follow, "pass1", "relay1", far_follow, first)

    when(has_down, lambda: got(exp_prev, "edge0"))
    when(has_up, lambda: got(exp_follow, "edge1"))

    def swap_edges(i, carry):
        at = pl.multiple_of(8 * i, 8)
        expo[i] = block_swap(exp_prev[pl.ds(at, 8), :])
        expo[38 + i] = block_swap(exp_follow[pl.ds(at, 8), :])
        return carry

    lax.fori_loop(0, 6, swap_edges, 0, unroll=2)
    got(r_core.at[4:16], "swap1")
    a_sum[4:16] = nums[c, 4:16] + r_core[4:16]

    spread = [remote(a_sum.at[chip(d) + 2], r_in.at[i], "rs1", there(d)) for i, d in enumerate(AWAY)]
    x_spread = [remote(a_sum.at[extra_pair(chip(d))], x_in.at[i], "x", there(d)) for i, d in enumerate(AWAY)]
    for d, copy in zip(AWAY, spread):
        when(jnp.logical_not(at_edge(chip(d))), copy.start)

    when(has_down, lambda: got(prev.at[1 - c], "pass0"))
    when(has_up, lambda: got(follow.at[1 - c], "pass1"))
    put(weave(prev, 0, 4), 0, mid, near)
    put(weave(follow, 0, 4), 320, mid, near)
    encode_rows(mid, near, code, 0, 0, 64)
    encode_rows(mid, near, code, 1, 0, 64)
    encode_rows(mid, near, code, 0, 320, 384)
    encode_rows(mid, near, code, 1, 304, 368)
    blurred = product(code, ((0, 8), (36, 8)), flip_hi, flip_lo)
    for low, source, count, weight, comes in (
        (0, 0, 6, w_down, has_down),
        (6, 48, 2, w_here, None),
        (36, 64, 2, w_here, None),
        (38, 80, 6, w_up, has_up),
    ):
        m = 8 * count
        value = weight * expo[low : low + count].reshape(m, 256) / blurred[source : source + m]
        if comes is not None:
            value = jnp.where(comes, value, 0.0)
        put(value, 8 * low, rmid, rnear)
    encode_rows(rmid, rnear, rcode, 0, 0, 64)
    encode_rows(rmid, rnear, rcode, 1, 0, 64)
    encode_rows(rmid, rnear, rcode, 0, 288, 352)
    encode_rows(rmid, rnear, rcode, 1, 272, 336)
    found = product(rcode, ((0, 8), (32, 8)), fwd_hi, fwd_lo).reshape(8, 2, 8, 256)
    for k in range(2):
        nums[k, 0:4] = found[0:4, k]
        nums[k, 16:20] = found[4:8, k]
    for at in (0, 16):
        remote(nums.at[1 - c, at : at + 4], r_core.at[at : at + 4], "swap2", partner).start()

    def normal(line):
        cover = iota((128, 256), 1) + iota((128, 256), 0) - 15
        valid = ((cover >= 0) & (cover < 256) & (iota((128, 256), 0) < 31)).astype(F32)
        return block_swap(jnp.dot(line, valid, precision=HI, preferred_element_type=F32))

    def total_of(own_part, parts):
        total = own_part
        for i in range(15):
            total = total + parts[i]
        return total

    got(q_in, "qsum")
    norm = normal(total_of(q_sum[u + 2], q_in))
    pair = jnp.where(extra, extra_pair(u), 0)

    @pl.when(extra)
    def _():
        got(qx_in, "qx")
        norms[...] = normal(total_of(q_sum[pair], qx_in))

    got(r_core.at[0:8], "swap2")
    for at in (0, 16):
        a_sum[at : at + 4] = nums[c, at : at + 4] + r_core[at : at + 4]
    for d, copy, x_copy in zip(AWAY, spread, x_spread):
        when(at_edge(chip(d)), copy.start)
        when(is_extra(chip(d)), x_copy.start)

    got(r_in, "rs1")
    model[c, u + 2] = own[c, u] * total_of(a_sum[u + 2], r_in) / norm

    mine = model.at[c, u + 2]
    arrival = jnp.where(late, ARRIVALS.index("ag2_late"), ARRIVALS.index("ag2_0") + z)
    for d in AWAY:
        remote(mine, mine, "ag2", there(d), arrival).start()

    @pl.when(late)
    def _():
        for d in AWAY + [(0, 0)]:
            remote(mine, mine, "ag2o", across(d)).start()

    @pl.when(extra)
    def _():
        got(x_in, "x")
        before = prev[c, jnp.where(u < 8, u - 4, 2)]
        after = follow[c, jnp.where(u < 8, 0, u - 8)]
        exists = jnp.where(u < 8, has_down.astype(jnp.int32), has_up.astype(jnp.int32)) > 0
        old = jnp.where(u < 8, before, after)
        new = old * total_of(a_sum[pair], x_in) / norms[...]
        model[c, pair] = jnp.where(exists, new, 0.0)
        block = model.at[c, pair]
        for d in AWAY:
            remote(block, block, "xg", there(d)).start()
        for d in AWAY + [(0, 0)]:
            remote(block, block, "xgo", across(d)).start()

    def got_all(ref, count, mine_too, name):
        when(mine_too, lambda: got(ref.at[c, 0 : count - 1], name))
        when(jnp.logical_not(mine_too), lambda: got(ref.at[c, 0:count], name))

    for row, low, high in ((1, 6, 10), (2, 10, 14), (0, 4, 6), (3, 14, 16)):
        got_all(model, high - low, (z == row) & jnp.logical_not(late), "ag2_%d" % row)
        part = model.at[c, low:high]
        remote(part, part, "hand2", partner).start()
    got(model.at[c, 0:12], "hand2")
    for g in range(3):
        put(weave(model, 4 + 4 * g, 4), 64 + 64 * g, mid, near)
    encode_rows(mid, near, code, 0, 64, 256)
    encode_rows(mid, near, code, 1, 64, 240)
    blurred = product(code, ((8, 20),), flip_hi, flip_lo)
    value = w_here * expo[12:32].reshape(160, 256) / blurred
    for g in range(5):
        put(value[32 * g : 32 * g + 32], 64 + 32 * g, rmid, rnear)
    encode_rows(rmid, rnear, rcode, 0, 64, 224)
    encode_rows(rmid, rnear, rcode, 1, 64, 208)
    found = product(rcode, ((8, 16),), fwd_hi, fwd_lo).reshape(8, 2, 8, 256)
    for k in range(2):
        nums2[k, 4:12] = found[:, k]
    remote(nums2.at[1 - c, 4:12], r_core2.at[4:12], "swap3", partner).start()
    got(r_core2.at[4:12], "swap3")
    a_sum2[4:12] = nums2[c, 4:12] + r_core2[4:12]
    spread = [remote(a_sum2.at[chip(d)], r_in2.at[i], "rs2", there(d)) for i, d in enumerate(AWAY)]

    def inner(place):
        return (place >= 4) & (place < 12)

    for d, copy in zip(AWAY, spread):
        when(inner(chip(d)), copy.start)

    got_all(model, 4, late, "ag2_late")
    got_all(model, 4, extra, "xg")
    got(model.at[c, 0:4], "ag2o")
    got(model.at[c, 0:4], "xgo")
    put(weave(model, 0, 4), 0, mid, near)
    put(weave(model, 16, 4), 256, mid, near)
    encode_rows(mid, near, code, 0, 0, 64)
    encode_rows(mid, near, code, 1, 0, 64)
    encode_rows(mid, near, code, 0, 256, 320)
    encode_rows(mid, near, code, 1, 240, 304)
    blurred = product(code, ((0, 8), (28, 8)), flip_hi, flip_lo)
    for low, source, count, weight, comes in (
        (0, 0, 2, w_down, has_down),
        (2, 16, 6, w_here, None),
        (28, 64, 6, w_here, None),
        (34, 112, 2, w_up, has_up),
    ):
        m = 8 * count
        value = weight * expo[low + 4 : low + 4 + count].reshape(m, 256) / blurred[source : source + m]
        if comes is not None:
            value = jnp.where(comes, value, 0.0)
        put(value, 8 * low, rmid, rnear)
    encode_rows(rmid, rnear, rcode, 0, 0, 64)
    encode_rows(rmid, rnear, rcode, 1, 0, 64)
    encode_rows(rmid, rnear, rcode, 0, 224, 288)
    encode_rows(rmid, rnear, rcode, 1, 208, 272)
    found = product(rcode, ((0, 8), (24, 8)), fwd_hi, fwd_lo).reshape(8, 2, 8, 256)
    for k in range(2):
        nums2[k, 0:4] = found[0:4, k]
        nums2[k, 12:16] = found[4:8, k]
    for at in (0, 12):
        remote(nums2.at[1 - c, at : at + 4], r_core2.at[at : at + 4], "swap4", partner).start()
    got(r_core2.at[0:8], "swap4")
    for at in (0, 12):
        a_sum2[at : at + 4] = nums2[c, at : at + 4] + r_core2[at : at + 4]
    for d, copy in zip(AWAY, spread):
        when(jnp.logical_not(inner(chip(d))), copy.start)
    got(r_in2, "rs2")
    out_ref[...] = block_swap(model[c, u + 2] * total_of(a_sum2[u], r_in2) / norm)

    for name in ("ag1", "rs1", "ag2", "rs2"):
        gone(r_in, name)
    gone(own.at[c], "hand1")
    gone(q_core, "qswap")
    gone(q_in, "qsum")
    gone(r_core.at[4:16], "swap1")
    gone(r_core.at[0:8], "swap2")
    gone(model.at[c, 0:12], "hand2")
    gone(r_core2.at[0:8], "swap3")
    gone(r_core2.at[0:8], "swap4")
    when(late, lambda: gone(r_core2, "ag2o"))
    when(extra, lambda: gone(r_core2, "xgo"))
    for ref, name in ((q_in, "qx"), (x_in, "x")):
        when(extra, lambda ref=ref, name=name: gone(ref.at[0:3], name))
        when(jnp.logical_not(extra), lambda ref=ref, name=name: gone(ref.at[0:4], name))
    when(extra, lambda: gone(x_in, "xg"))
    when(has_up, lambda: gone(exp_prev, "edge0"))
    when(has_down, lambda: gone(exp_follow, "edge1"))
    when(last & has_up, lambda: gone(prev.at[c, 0], "hop0"))
    when(first & has_down, lambda: gone(prev.at[c, 0], "hop1"))
    when(last & has_down, lambda: gone(x_in, "relay0"))
    when(first & has_up, lambda: gone(x_in, "relay1"))
    when(has_down, lambda: gone(prev.at[c], "pass0"))
    when(has_up, lambda: gone(prev.at[c], "pass1"))


def body(exposures, sky_model, blur_kernels, coverage):
    vmem = pl.BlockSpec(memory_space=pltpu.VMEM)
    V = pltpu.VMEM
    D = pltpu.SemaphoreType.DMA
    op = V((7, 2, 8, 32, 256), BF)

    def blocks(*dims):
        return V((*dims, 8, 256), F32)

    def lanes(*dims):
        return V((*dims, 8, 128), F32)

    return pl.pallas_call(
        kernel,
        out_shape=jax.ShapeDtypeStruct((8, 256), F32),
        in_specs=[pl.BlockSpec(memory_space=pl.ANY)] * 4,
        out_specs=vmem,
        scratch_shapes=[
            V((256, 256), F32), V((8, 256), F32), V((31, 1, 31), F32), pltpu.SMEM((1, 8), jnp.int32),
            V((32, 128), F32), V((48, 128), F32), op, op, op, op,
            V((384, 256), F32), V((384, 256), F32), V((352, 256), F32), V((352, 256), F32),
            V((2, 2, 384, 512), BF), V((2, 2, 352, 512), BF),
            blocks(2, 16), blocks(2, 4), blocks(2, 4), blocks(2, 20), V((48, 256), F32), V((48, 256), F32), blocks(44),
            V((8, 256), F32),
            lanes(2, 20), lanes(20), lanes(20), lanes(15), lanes(15),
            blocks(2, 20), blocks(20), blocks(20), blocks(15), blocks(15), blocks(2, 16), blocks(16), blocks(16), blocks(15),
            D((4,)), D((len(SENDS),)), D((len(ARRIVALS),)),
        ],
        compiler_params=pltpu.CompilerParams(collective_id=0, has_side_effects=True),
    )(exposures, sky_model, jnp.transpose(blur_kernels, (1, 0, 2)), coverage)


def solution(mesh):
    return jax.shard_map(
        body,
        mesh=mesh,
        in_specs=(
            P("visit", "tile", None),
            P(("tile", "visit"), None),
            P("visit", None, None),
            P("visit", None),
        ),
        out_specs=P(("tile", "visit"), None),
        check_vma=False,
    )
```

```python
import jax
import jax.numpy as jnp
from jax import lax
from jax.experimental import pallas as pl
from jax.experimental.pallas import tpu as pltpu
from jax.sharding import PartitionSpec as P

F32 = jnp.float32
BF = jnp.bfloat16
HI = lax.Precision.HIGHEST
MESH = pl.DeviceIdType.MESH
ITERS = 2


def iota(shape, dim):
    return lax.broadcasted_iota(jnp.int32, shape, dim)


def block_swap(x):
    s = iota((8, 256), 0)
    b = iota((8, 256), 1) // 32
    out = x
    for d in range(1, 8):
        moved = pltpu.roll(pltpu.roll(x, d, 0), 256 - 32 * d, 1)
        out = jnp.where((s - b) % 8 == d, moved, out)
    return out


def build_rows(k, rows):
    rows[...] = jnp.zeros_like(rows)
    m = iota((128, 128), 1)
    b = iota((128, 128), 0)
    for r in range(4):
        pick = ((m == (32 * r - 1 - b + 256) % 128) & (b < 31)).astype(F32)
        moved = jnp.dot(k, pick, precision=HI, preferred_element_type=F32)
        rows[5 + r : 37 + r, :] = rows[5 + r : 37 + r, :] + moved


def build_operator(rows, op_hi, op_lo):
    c2 = iota((64, 128), 0)
    b = c2 - 1 - iota((64, 128), 1) % 32
    inside = (b >= 0) & (b <= 30)

    def step(j, carry):
        wide = jnp.broadcast_to(rows[pl.ds(j, 1), :], (8, 128))
        base = pltpu.roll(wide, 0, 1, stride=1, stride_axis=0)
        value = jnp.concatenate([base] + [pltpu.roll(base, 8 * i, 1) for i in range(1, 8)], axis=0)
        value = jnp.where(inside, value, 0.0)
        hi = value.astype(BF)
        lo = (value - hi.astype(F32)).astype(BF)
        for shift, lanes in ((4, slice(0, 128)), (8, slice(128, 256))):
            o, r = (j + shift) // 8, (j + shift) % 8
            for op, x in ((op_hi, hi), (op_lo, lo)):
                op[o, 0, r, :, lanes] = x[16:48]
                op[o, 1, r, 0:16, lanes] = x[48:64]
                op[o, 1, r, 16:32, lanes] = x[0:16]
        return carry

    lax.fori_loop(0, 44, step, 0, unroll=11)


def beside(value):
    n = value.shape[0]
    group = iota(value.shape, 0) % 8
    before = jnp.where(group > 0, pltpu.roll(value, 1, 0), 0.0)
    after = jnp.where(group < 7, pltpu.roll(value, n - 1, 0), 0.0)
    return jnp.where(iota(value.shape, 1) % 32 < 16, after, before)


def put(value, first, mid, near):
    n = value.shape[0]
    mid[first : first + n, :] = value
    near[first : first + n, :] = beside(value)


def weave(ref, first, count):
    pairs = [ref[0, first : first + count], ref[1, first : first + count]]
    return jnp.stack(pairs, axis=1).reshape(16 * count, 256)


def encode(value, code, rows, lanes):
    hi = value.astype(BF)
    code[0, rows, lanes] = hi
    code[1, rows, lanes] = (value - hi.astype(F32)).astype(BF)


def encode_rows(mid, near, code, shift, first, last):
    for at in range(first, last, 64):
        n = min(64, last - at)
        for k, src in ((0, mid), (1, near)):
            rows = slice(at + 8 * shift, at + 8 * shift + n)
            encode(src[rows, :], code.at[shift], slice(at, at + n), slice(256 * k, 256 * k + 256))


def multiply(left, op_hi, op_lo):
    def dot(x, op):
        return jnp.dot(x, op[1:6].reshape(2560, 256), preferred_element_type=F32)

    hi, lo = left
    return dot(hi, op_hi) + (dot(hi, op_lo) + dot(lo, op_hi))


def product(code, ranges, op_hi, op_lo):
    left = []
    for term in range(2):
        parts = []
        for first, count in ranges:
            at = [8 * first + 16 * (o // 2) for o in range(5)]
            parts.append(
                jnp.concatenate([code[o % 2, term, at[o] : at[o] + 8 * count, :] for o in range(5)], axis=1)
            )
        left.append(jnp.concatenate(parts, axis=0) if len(parts) > 1 else parts[0])
    return multiply(left, op_hi, op_lo)


def far(d):
    return -(d[0] + (2 if d[1] == 2 else 1 if d[1] else 0))


AWAY = sorted([(dz, dy) for dz in range(4) for dy in range(4) if (dz, dy) != (0, 0)], key=far)
SENDS = ("ag1", "hand1", "qswap", "qsum", "qx", "swap1", "swap2", "rs1", "x", "ag2", "hand2", "xg", "swap3", "rs2")
SENDS += ("ag2o", "xgo", "swap4", "hop0", "hop1", "relay0", "relay1", "pass0", "pass1", "edge0", "edge1")
ARRIVALS = ("ag1_0", "ag1_1", "ag1_2", "ag1_3", "ag2_0", "ag2_1", "ag2_2", "ag2_3", "ag2_late") + SENDS


def is_extra(u):
    return (u >= 6) & (u < 10)


def extra_pair(u):
    return jnp.where(u < 8, u - 6, u + 10)


def kernel(
    exp_hbm, sky_hbm, ker_hbm, cov_hbm, out_ref,
    exp_ref, sky_ref, ker_ref, cov_ref, kpad, rows, fwd_hi, fwd_lo, flip_hi, flip_lo, mid, near, rmid, rnear, code, rcode,
    own, prev, follow, model, exp_prev, exp_follow, expo, norms,
    q_all, q_core, q_sum, q_in, qx_in, nums, r_core, a_sum, r_in, x_in, nums2, r_core2, a_sum2, r_in2,
    load_sems, send_sems, recv_sems,
):
    t = lax.axis_index("tile")
    v = lax.axis_index("visit")
    tiles = lax.axis_size("tile")
    z, y, c = v // 8, (v // 2) % 4, v % 2
    u = v // 2

    def chip(d):
        return ((z + d[0]) % 4) * 4 + (y + d[1]) % 4

    def there(d):
        return {"visit": 2 * chip(d) + c, "tile": t}

    partner = {"visit": 2 * u + (1 - c), "tile": t}
    up = {"visit": v, "tile": t + 1}
    down = {"visit": v, "tile": t - 1}
    has_up = t < tiles - 1
    has_down = t > 0
    extra = is_extra(u)

    def at_edge(place):
        return (place < 2) | (place >= 14)

    late = at_edge(u)

    loads = [
        pltpu.make_async_copy(src, dst, load_sems.at[i])
        for i, (src, dst) in enumerate(
            ((ker_hbm, ker_ref), (cov_hbm, cov_ref), (sky_hbm, sky_ref), (exp_hbm.at[0], exp_ref))
        )
    ]
    for copy in loads:
        copy.start()
    prev[...] = jnp.zeros_like(prev)
    follow[...] = jnp.zeros_like(follow)
    barrier = pltpu.get_barrier_semaphore()
    for peer in [there(d) for d in AWAY] + [partner]:
        pl.semaphore_signal(barrier, inc=1, device_id=peer, device_id_type=MESH)

    @pl.when(has_up)
    def _():
        pl.semaphore_signal(barrier, inc=1, device_id=up, device_id_type=MESH)

    @pl.when(has_down)
    def _():
        pl.semaphore_signal(barrier, inc=1, device_id=down, device_id_type=MESH)

    def remote(src, dst, name, device, arrival=None):
        return pltpu.make_async_remote_copy(
            src_ref=src,
            dst_ref=dst,
            send_sem=send_sems.at[SENDS.index(name)],
            recv_sem=recv_sems.at[ARRIVALS.index(name) if arrival is None else arrival],
            device_id=device,
            device_id_type=MESH,
        )

    def got(ref, name):
        remote(ref, ref, "ag1", partner, ARRIVALS.index(name)).wait_recv()

    def gone(ref, name):
        remote(ref, ref, name, partner).wait_send()

    def when(cond, act):
        pl.when(cond)(act)

    kpad[...] = jnp.zeros_like(kpad)
    loads[0].wait()
    raw = ker_ref[:, 0, :]
    kpad[0:31, 0:31] = raw / jnp.sum(raw)
    loads[1].wait()
    w_here = cov_ref[0, t].astype(F32)
    w_down = jnp.where(has_down, cov_ref[0, jnp.maximum(t - 1, 0)], 0).astype(F32)
    w_up = jnp.where(has_up, cov_ref[0, jnp.minimum(t + 1, tiles - 1)], 0).astype(F32)
    i128, a32 = iota((128, 32), 0), iota((128, 32), 1)
    weights = jnp.where(
        i128 < 64,
        jnp.where(i128 + a32 < 47, w_down, w_here),
        jnp.where(i128 + a32 >= 111, w_up, w_here),
    )
    lines = jnp.dot(weights, kpad[...], precision=HI, preferred_element_type=F32)
    for b in range(40):
        at = 8 * b if b < 8 else 64 + 8 * (b - 32) if b >= 32 else 48
        q_all[b % 2, b // 2] = lines[at : at + 8]
    loads[2].wait()
    own[c, u] = block_swap(sky_ref[...])
    turn_rows = (iota((32, 32), 0) + iota((32, 32), 1) == 30).astype(F32)
    turn_cols = (iota((128, 128), 0) + iota((128, 128), 1) == 30).astype(F32)
    turned = jnp.dot(turn_rows, kpad[...], precision=HI, preferred_element_type=F32)
    turned = jnp.dot(turned, turn_cols, precision=HI, preferred_element_type=F32)
    build_rows(turned, rows)
    build_operator(rows, flip_hi, flip_lo)

    pl.semaphore_wait(barrier, 16 + has_up.astype(jnp.int32) + has_down.astype(jnp.int32))

    edge_up = remote(exp_ref.at[208:256, :], exp_prev, "edge0", up)
    edge_down = remote(exp_ref.at[0:48, :], exp_follow, "edge1", down)
    mine = own.at[c, u]
    hop_up = remote(mine, prev.at[c, u % 4], "hop0", up)
    hop_down = remote(mine, follow.at[c, u % 4], "hop1", down)
    last = u >= 12
    first = u < 4

    def relay_up():
        got(prev.at[c, u % 4], "hop0")
        block = prev.at[c, u % 4]
        for d in AWAY:
            remote(block, block, "relay0", there(d)).start()

    def relay_down():
        got(follow.at[c, u % 4], "hop1")
        block = follow.at[c, u % 4]
        for d in AWAY:
            remote(block, block, "relay1", there(d)).start()

    def hand_over(halo, name, relayed, comes, relayer):
        when(comes & relayer, lambda: got(halo.at[c, 0:3], relayed))
        when(comes & jnp.logical_not(relayer), lambda: got(halo.at[c], relayed))
        when(comes, lambda: remote(halo.at[c], halo.at[c], name, partner).start())

    when(last & has_up, hop_up.start)
    when(first & has_down, hop_down.start)
    for d in AWAY:
        remote(mine, mine, "ag1", there(d), z).start()
    remote(q_all.at[1 - c], q_core, "qswap", partner).start()
    loads[3].wait()
    when(has_up, edge_up.start)
    when(has_down, edge_down.start)
    build_rows(kpad[...], rows)
    build_operator(rows, fwd_hi, fwd_lo)
    when(last & has_down, relay_up)
    when(first & has_up, relay_down)

    def swap_exposure(i, carry):
        for j in range(4):
            at = pl.multiple_of(32 * i + 8 * j, 8)
            expo[4 * i + j + 6] = block_swap(exp_ref[pl.ds(at, 8), :])
        return carry

    lax.fori_loop(0, 8, swap_exposure, 0)

    def got_row(ref, row, name):
        when(z == row, lambda: got(ref.at[c, 0:3], name))
        when(z != row, lambda: got(ref.at[c, 0:4], name))

    for row in (1, 2, 0, 3):
        got_row(own, row, "ag1_%d" % row)
        part = own.at[c, 4 * row : 4 * row + 4]
        remote(part, part, "hand1", partner).start()
    got(own.at[c], "hand1")

    for g in range(4):
        put(weave(own, 4 * g, 4), 64 + 64 * g, mid, near)
    encode_rows(mid, near, code, 0, 64, 320)
    encode_rows(mid, near, code, 1, 64, 304)
    blurred = product(code, ((8, 28),), flip_hi, flip_lo)
    value = w_here * expo[8:36].reshape(224, 256) / blurred
    for g in range(7):
        put(value[32 * g : 32 * g + 32], 64 + 32 * g, rmid, rnear)
    encode_rows(rmid, rnear, rcode, 0, 64, 288)
    encode_rows(rmid, rnear, rcode, 1, 64, 272)

    got(q_core, "qswap")
    q_sum[...] = q_all[c] + q_core[...]
    for i, d in enumerate(AWAY):
        remote(q_sum.at[chip(d) + 2], q_in.at[i], "qsum", there(d)).start()
    for i, d in enumerate(AWAY):
        when(is_extra(chip(d)), remote(q_sum.at[extra_pair(chip(d))], qx_in.at[i], "qx", there(d)).start)

    far_prev = t == tiles // 2
    far_follow = t == tiles // 2 - 1
    hand_over(prev, "pass0", "relay0", has_down & jnp.logical_not(far_prev), last)
    hand_over(follow, "pass1", "relay1", has_up & jnp.logical_not(far_follow), first)
    found = product(rcode, ((8, 24),), fwd_hi, fwd_lo).reshape(12, 2, 8, 256)
    for k in range(2):
        nums[k, 4:16] = found[:, k]
    remote(nums.at[1 - c, 4:16], r_core.at[4:16], "swap1", partner).start()
    hand_over(prev, "pass0", "relay0", far_prev, last)
    hand_over(follow, "pass1", "relay1", far_follow, first)

    when(has_down, lambda: got(exp_prev, "edge0"))
    when(has_up, lambda: got(exp_follow, "edge1"))

    def swap_edges(i, carry):
        at = pl.multiple_of(8 * i, 8)
        expo[i] = block_swap(exp_prev[pl.ds(at, 8), :])
        expo[38 + i] = block_swap(exp_follow[pl.ds(at, 8), :])
        return carry

    lax.fori_loop(0, 6, swap_edges, 0, unroll=2)
    got(r_core.at[4:16], "swap1")
    a_sum[4:16] = nums[c, 4:16] + r_core[4:16]

    spread = [remote(a_sum.at[chip(d) + 2], r_in.at[i], "rs1", there(d)) for i, d in enumerate(AWAY)]
    x_spread = [remote(a_sum.at[extra_pair(chip(d))], x_in.at[i], "x", there(d)) for i, d in enumerate(AWAY)]
    for d, copy in zip(AWAY, spread):
        when(jnp.logical_not(at_edge(chip(d))), copy.start)

    when(has_down, lambda: got(prev.at[1 - c], "pass0"))
    when(has_up, lambda: got(follow.at[1 - c], "pass1"))
    put(weave(prev, 0, 4), 0, mid, near)
    put(weave(follow, 0, 4), 320, mid, near)
    encode_rows(mid, near, code, 0, 0, 64)
    encode_rows(mid, near, code, 1, 0, 64)
    encode_rows(mid, near, code, 0, 320, 384)
    encode_rows(mid, near, code, 1, 304, 368)
    blurred = product(code, ((0, 8), (36, 8)), flip_hi, flip_lo)
    for low, source, count, weight, comes in (
        (0, 0, 6, w_down, has_down),
        (6, 48, 2, w_here, None),
        (36, 64, 2, w_here, None),
        (38, 80, 6, w_up, has_up),
    ):
        m = 8 * count
        value = weight * expo[low : low + count].reshape(m, 256) / blurred[source : source + m]
        if comes is not None:
            value = jnp.where(comes, value, 0.0)
        put(value, 8 * low, rmid, rnear)
    encode_rows(rmid, rnear, rcode, 0, 0, 64)
    encode_rows(rmid, rnear, rcode, 1, 0, 64)
    encode_rows(rmid, rnear, rcode, 0, 288, 352)
    encode_rows(rmid, rnear, rcode, 1, 272, 336)
    found = product(rcode, ((0, 8), (32, 8)), fwd_hi, fwd_lo).reshape(8, 2, 8, 256)
    for k in range(2):
        nums[k, 0:4] = found[0:4, k]
        nums[k, 16:20] = found[4:8, k]
    for at in (0, 16):
        remote(nums.at[1 - c, at : at + 4], r_core.at[at : at + 4], "swap2", partner).start()

    def normal(line):
        cover = iota((128, 256), 1) + iota((128, 256), 0) - 15
        valid = ((cover >= 0) & (cover < 256) & (iota((128, 256), 0) < 31)).astype(F32)
        return block_swap(jnp.dot(line, valid, precision=HI, preferred_element_type=F32))

    def total_of(own_part, parts):
        total = own_part
        for i in range(15):
            total = total + parts[i]
        return total

    got(q_in, "qsum")
    norm = normal(total_of(q_sum[u + 2], q_in))
    pair = jnp.where(extra, extra_pair(u), 0)

    @pl.when(extra)
    def _():
        got(qx_in, "qx")
        norms[...] = normal(total_of(q_sum[pair], qx_in))

    got(r_core.at[0:8], "swap2")
    for at in (0, 16):
        a_sum[at : at + 4] = nums[c, at : at + 4] + r_core[at : at + 4]
    for d, copy, x_copy in zip(AWAY, spread, x_spread):
        when(at_edge(chip(d)), copy.start)
        when(is_extra(chip(d)), x_copy.start)

    got(r_in, "rs1")
    model[c, u + 2] = own[c, u] * total_of(a_sum[u + 2], r_in) / norm

    mine = model.at[c, u + 2]
    arrival = jnp.where(late, ARRIVALS.index("ag2_late"), ARRIVALS.index("ag2_0") + z)
    for d in AWAY:
        remote(mine, mine, "ag2", there(d), arrival).start()

    @pl.when(extra)
    def _():
        got(x_in, "x")
        before = prev[c, jnp.where(u < 8, u - 4, 2)]
        after = follow[c, jnp.where(u < 8, 0, u - 8)]
        exists = jnp.where(u < 8, has_down.astype(jnp.int32), has_up.astype(jnp.int32)) > 0
        old = jnp.where(u < 8, before, after)
        new = old * total_of(a_sum[pair], x_in) / norms[...]
        model[c, pair] = jnp.where(exists, new, 0.0)
        block = model.at[c, pair]
        for d in AWAY:
            remote(block, block, "xg", there(d)).start()

    def got_all(ref, count, mine_too, name):
        when(mine_too, lambda: got(ref.at[c, 0 : count - 1], name))
        when(jnp.logical_not(mine_too), lambda: got(ref.at[c, 0:count], name))

    for row, low, high in ((1, 6, 10), (2, 10, 14), (0, 4, 6), (3, 14, 16)):
        got_all(model, high - low, (z == row) & jnp.logical_not(late), "ag2_%d" % row)
        part = model.at[c, low:high]
        remote(part, part, "hand2", partner).start()
    got(model.at[c, 0:12], "hand2")
    for g in range(3):
        put(weave(model, 4 + 4 * g, 4), 64 + 64 * g, mid, near)
    encode_rows(mid, near, code, 0, 64, 256)
    encode_rows(mid, near, code, 1, 64, 240)
    blurred = product(code, ((8, 20),), flip_hi, flip_lo)
    value = w_here * expo[12:32].reshape(160, 256) / blurred
    for g in range(5):
        put(value[32 * g : 32 * g + 32], 64 + 32 * g, rmid, rnear)
    encode_rows(rmid, rnear, rcode, 0, 64, 224)
    encode_rows(rmid, rnear, rcode, 1, 64, 208)
    found = product(rcode, ((8, 16),), fwd_hi, fwd_lo).reshape(8, 2, 8, 256)
    for k in range(2):
        nums2[k, 4:12] = found[:, k]
    remote(nums2.at[1 - c, 4:12], r_core2.at[4:12], "swap3", partner).start()
    got_all(model, 4, late, "ag2_late")
    got_all(model, 4, extra, "xg")
    for name, at in (("ag2o", 0), ("xgo", 16)):
        part = model.at[c, at : at + 4]
        remote(part, part, name, partner).start()
    got(r_core2.at[4:12], "swap3")
    a_sum2[4:12] = nums2[c, 4:12] + r_core2[4:12]
    spread = [remote(a_sum2.at[chip(d)], r_in2.at[i], "rs2", there(d)) for i, d in enumerate(AWAY)]

    def inner(place):
        return (place >= 4) & (place < 12)

    for d, copy in zip(AWAY, spread):
        when(inner(chip(d)), copy.start)

    got(model.at[c, 0:4], "ag2o")
    got(model.at[c, 0:4], "xgo")
    put(weave(model, 0, 4), 0, mid, near)
    put(weave(model, 16, 4), 256, mid, near)
    encode_rows(mid, near, code, 0, 0, 64)
    encode_rows(mid, near, code, 1, 0, 64)
    encode_rows(mid, near, code, 0, 256, 320)
    encode_rows(mid, near, code, 1, 240, 304)
    blurred = product(code, ((0, 8), (28, 8)), flip_hi, flip_lo)
    for low, source, count, weight, comes in (
        (0, 0, 2, w_down, has_down),
        (2, 16, 6, w_here, None),
        (28, 64, 6, w_here, None),
        (34, 112, 2, w_up, has_up),
    ):
        m = 8 * count
        value = weight * expo[low + 4 : low + 4 + count].reshape(m, 256) / blurred[source : source + m]
        if comes is not None:
            value = jnp.where(comes, value, 0.0)
        put(value, 8 * low, rmid, rnear)
    encode_rows(rmid, rnear, rcode, 0, 0, 64)
    encode_rows(rmid, rnear, rcode, 1, 0, 64)
    encode_rows(rmid, rnear, rcode, 0, 224, 288)
    encode_rows(rmid, rnear, rcode, 1, 208, 272)
    found = product(rcode, ((0, 8), (24, 8)), fwd_hi, fwd_lo).reshape(8, 2, 8, 256)
    for k in range(2):
        nums2[k, 0:4] = found[0:4, k]
        nums2[k, 12:16] = found[4:8, k]
    for at in (0, 12):
        remote(nums2.at[1 - c, at : at + 4], r_core2.at[at : at + 4], "swap4", partner).start()
    got(r_core2.at[0:8], "swap4")
    for at in (0, 12):
        a_sum2[at : at + 4] = nums2[c, at : at + 4] + r_core2[at : at + 4]
    for d, copy in zip(AWAY, spread):
        when(jnp.logical_not(inner(chip(d))), copy.start)
    got(r_in2, "rs2")
    out_ref[...] = block_swap(model[c, u + 2] * total_of(a_sum2[u], r_in2) / norm)

    for name in ("ag1", "rs1", "ag2", "rs2"):
        gone(r_in, name)
    gone(own.at[c], "hand1")
    gone(q_core, "qswap")
    gone(q_in, "qsum")
    gone(r_core.at[4:16], "swap1")
    gone(r_core.at[0:8], "swap2")
    gone(model.at[c, 0:12], "hand2")
    gone(r_core2.at[0:8], "swap3")
    gone(r_core2.at[0:8], "swap4")
    gone(model.at[c, 0:4], "ag2o")
    gone(model.at[c, 0:4], "xgo")
    for ref, name in ((q_in, "qx"), (x_in, "x")):
        when(extra, lambda ref=ref, name=name: gone(ref.at[0:3], name))
        when(jnp.logical_not(extra), lambda ref=ref, name=name: gone(ref.at[0:4], name))
    when(extra, lambda: gone(x_in, "xg"))
    when(has_up, lambda: gone(exp_prev, "edge0"))
    when(has_down, lambda: gone(exp_follow, "edge1"))
    when(last & has_up, lambda: gone(prev.at[c, 0], "hop0"))
    when(first & has_down, lambda: gone(prev.at[c, 0], "hop1"))
    when(last & has_down, lambda: gone(x_in, "relay0"))
    when(first & has_up, lambda: gone(x_in, "relay1"))
    when(has_down, lambda: gone(prev.at[c], "pass0"))
    when(has_up, lambda: gone(prev.at[c], "pass1"))


def body(exposures, sky_model, blur_kernels, coverage):
    vmem = pl.BlockSpec(memory_space=pltpu.VMEM)
    V = pltpu.VMEM
    D = pltpu.SemaphoreType.DMA
    op = V((7, 2, 8, 32, 256), BF)

    def blocks(*dims):
        return V((*dims, 8, 256), F32)

    def lanes(*dims):
        return V((*dims, 8, 128), F32)

    return pl.pallas_call(
        kernel,
        out_shape=jax.ShapeDtypeStruct((8, 256), F32),
        in_specs=[pl.BlockSpec(memory_space=pl.ANY)] * 4,
        out_specs=vmem,
        scratch_shapes=[
            V((256, 256), F32), V((8, 256), F32), V((31, 1, 31), F32), pltpu.SMEM((1, 8), jnp.int32),
            V((32, 128), F32), V((48, 128), F32), op, op, op, op,
            V((384, 256), F32), V((384, 256), F32), V((352, 256), F32), V((352, 256), F32),
            V((2, 2, 384, 512), BF), V((2, 2, 352, 512), BF),
            blocks(2, 16), blocks(2, 4), blocks(2, 4), blocks(2, 20), V((48, 256), F32), V((48, 256), F32), blocks(44),
            V((8, 256), F32),
            lanes(2, 20), lanes(20), lanes(20), lanes(15), lanes(15),
            blocks(2, 20), blocks(20), blocks(20), blocks(15), blocks(15), blocks(2, 16), blocks(16), blocks(16), blocks(15),
            D((4,)), D((len(SENDS),)), D((len(ARRIVALS),)),
        ],
        compiler_params=pltpu.CompilerParams(collective_id=0, has_side_effects=True),
    )(exposures, sky_model, jnp.transpose(blur_kernels, (1, 0, 2)), coverage)


def solution(mesh):
    return jax.shard_map(
        body,
        mesh=mesh,
        in_specs=(
            P("visit", "tile", None),
            P(("tile", "visit"), None),
            P("visit", None, None),
            P("visit", None),
        ),
        out_specs=P(("tile", "visit"), None),
        check_vma=False,
    )
```
